32 devices in a mesh: groups: 2 (over y), seq: 16 (over z, x, core).
Axes of the slice: x: 2, y: 2, z: 4, core: 2. Of those that a mesh axis runs over, the one named last changes fastest.
Arguments:
- query_rows: bfloat16 [8192, 8, 128], P(('groups', 'seq')), parts along dimension 0, may hold values from -48 to 48
- key_rows: bfloat16 [8192, 8, 128], P(('groups', 'seq')), parts along dimension 0, may hold values from -7 to 7
- value_rows: bfloat16 [8192, 8, 128], P(('groups', 'seq')), parts along dimension 0, may hold values from -6 to 6
- out_grad: bfloat16 [8192, 8, 128], P(('groups', 'seq')), parts along dimension 0, may hold values from -6 to 6
Outputs:
- attended: bfloat16 [8192, 8, 128], P(('groups', 'seq')), parts along dimension 0
- query_grad: bfloat16 [8192, 8, 128], P(('groups', 'seq')), parts along dimension 0
- key_grad: bfloat16 [8192, 8, 128], P(('groups', 'seq')), parts along dimension 0
- value_grad: bfloat16 [8192, 8, 128], P(('groups', 'seq')), parts along dimension 0
The draws below stay inside these ranges and needn't reach their ends.
There are 2 independent parts, one for each index of `groups`. The reference program is written for one: setup_inputs(seed, part) draws one part's arguments, and reference() takes and returns one part's arrays. A program takes and returns all parts, laid end to end along the dimension named above; each array names one. Nothing has to cross between parts.
All inputs are finite; a program needn't handle non-finite values.
Results may differ from the reference program's by a relative error of at most 0.018.
Values may be sent and summed in bfloat16 or wider, within the bound.
A program may use at most 128 MiB of HBM per device.

```python
from functools import partial
import jax
import jax.numpy as jnp
from jax import lax

HEADS = 8
HDIM = 128
BLOCK = 128
TOKENS = 4096


def layered(key, stream):
    dims = (TOKENS, HEADS, HDIM)
    summed = jnp.zeros(dims, jnp.float32)
    top_exponent = TOKENS.bit_length() - 1
    for exponent in range(4, top_exponent - 2):
        run_shape = (TOKENS >> exponent, HEADS, HDIM)
        sub_key = jax.random.fold_in(key, stream + exponent)
        run_values = jax.random.truncated_normal(sub_key, -3.0, 3.0, run_shape, jnp.float32)
        summed = summed + jnp.repeat(run_values, 1 << exponent, axis=0)
    return summed


def drawn_noise(key, stream, spread, shaped):
    sub_key = jax.random.fold_in(key, stream)
    return spread * jax.random.truncated_normal(sub_key, -3.0, 3.0, shaped, jnp.float32)


def joint_pair(key):
    dims = (TOKENS, HEADS, HDIM)
    base_keys = drawn_noise(key, 11, 0.8, dims) + 0.35 * layered(key, 100)
    base_query = drawn_noise(key, 12, 2.0, dims) + layered(key, 200)
    return (jnp.clip(base_query, -48.0, 48.0), jnp.clip(base_keys, -7.0, 7.0))


def draw_query_rows(key, part):
    return joint_pair(key)[0].astype(jnp.bfloat16)


def draw_key_rows(key, part):
    return joint_pair(key)[1].astype(jnp.bfloat16)


def draw_value_rows(key, part):
    dims = (TOKENS, HEADS, HDIM)
    shift = jax.random.uniform(jax.random.fold_in(key, 21), (1, HEADS, HDIM), jnp.float32, -1.0, 1.0)
    field = drawn_noise(key, 22, 0.8, dims) + 0.3 * layered(key, 300) + shift
    return jnp.clip(field, -6.0, 6.0).astype(jnp.bfloat16)


def draw_out_grad(key, part):
    dims = (TOKENS, HEADS, HDIM)
    common = 0.8 * jax.random.truncated_normal(jax.random.fold_in(key, 31), -3.0, 3.0, (1, HEADS, HDIM), jnp.float32)
    field = drawn_noise(key, 32, 0.8, dims) + 0.25 * layered(key, 400) + common
    return jnp.clip(field, -6.0, 6.0).astype(jnp.bfloat16)


def setup_inputs(seed: int = 0, part: int = 0) -> dict:
    key_of = jax.random.split(jax.random.key(seed), 5)
    own_keys = jax.random.split(jax.random.fold_in(key_of[4], part), 5)
    query_rows = draw_query_rows(jax.random.fold_in(jax.random.fold_in(key_of[4], part), 71), part)
    key_rows = draw_key_rows(jax.random.fold_in(jax.random.fold_in(key_of[4], part), 71), part)
    value_rows = draw_value_rows(jax.random.fold_in(jax.random.fold_in(key_of[4], part), 71), part)
    out_grad = draw_out_grad(jax.random.fold_in(jax.random.fold_in(key_of[4], part), 71), part)
    return {"query_rows": query_rows, "key_rows": key_rows, "value_rows": value_rows, "out_grad": out_grad}


def keep_round(values):
    frozen = lax.stop_gradient(values)
    lowered = lax.optimization_barrier(frozen.astype(jnp.bfloat16))
    return values + (lowered.astype(values.dtype) - frozen)

def coarsen(fields, height):
    if height == 0:
        return fields
    row_count = fields.shape[0] >> height
    grouped = fields.reshape((row_count, 1 << height) + fields.shape[1:])
    return keep_round(lax.optimization_barrier(jnp.mean(grouped, axis=1)))

def block_term(weight, query_blocks, key_blocks, value_blocks):
    factor = query_blocks.shape[-1] ** (-0.5)
    scores = jnp.einsum('bqhd,bkhd->bqhk', query_blocks, key_blocks, precision=lax.Precision.HIGHEST) * factor
    row_max = lax.stop_gradient(lax.optimization_barrier(jnp.max(scores, axis=-1)))
    weights = jnp.exp(scores - row_max[..., None])
    denominator = weight * lax.optimization_barrier(jnp.sum(weights, axis=-1))
    numerator = weight * jnp.einsum('bqhk,bkhd->bqhd', keep_round(weights), value_blocks, precision=lax.Precision.HIGHEST)
    row_count = query_blocks.shape[0] * query_blocks.shape[1]
    return (row_max.reshape((row_count,) + row_max.shape[2:]), denominator.reshape((row_count,) + denominator.shape[2:]), numerator.reshape((row_count,) + numerator.shape[2:]))

def combine(earlier, second):
    row_max = jnp.maximum(earlier[0], second[0])
    scale_a = jnp.exp(earlier[0] - row_max)
    scale_b = jnp.exp(second[0] - row_max)
    return (row_max, scale_a * earlier[1] + scale_b * second[1], scale_a[..., None] * earlier[2] + scale_b[..., None] * second[2])

def upsample(summary):
    return tuple((jnp.repeat(entry, 2, axis=0) for entry in summary))

def flip_pairs(blocks):
    paired = blocks.reshape((blocks.shape[0] // 2, 2) + blocks.shape[1:])
    return paired[:, ::-1].reshape(blocks.shape)

def attend(query32, key32, value32):
    block_count = query32.shape[0] // BLOCK
    levels = block_count.bit_length() - 1
    summary = None
    for height in reversed(range(levels)):
        nblocks = block_count >> height
        block_shape = (nblocks, BLOCK) + query32.shape[1:]
        query_c = coarsen(query32, height).reshape(block_shape)
        keys_c = flip_pairs(coarsen(key32, height).reshape(block_shape))
        values_c = flip_pairs(coarsen(value32, height).reshape(block_shape))
        partial_term = jax.checkpoint(partial(block_term, float(1 << height)))(query_c, keys_c, values_c)
        summary = partial_term if summary is None else combine(upsample(summary), partial_term)
    block_shape = (block_count, BLOCK) + query32.shape[1:]
    diagonal = jax.checkpoint(partial(block_term, 1.0))(query32.reshape(block_shape), key32.reshape(block_shape), value32.reshape(block_shape))
    summary = combine(summary, diagonal)
    return summary[2] / summary[1][..., None]

def reference(query_rows, key_rows, value_rows, out_grad):
    attention, pullback = jax.vjp(attend, query_rows.astype(jnp.float32), key_rows.astype(jnp.float32), value_rows.astype(jnp.float32))
    grads = pullback(out_grad.astype(jnp.float32))
    return (attention.astype(jnp.bfloat16), grads[0].astype(jnp.bfloat16), grads[1].astype(jnp.bfloat16), grads[2].astype(jnp.bfloat16))
```

```python
from functools import partial
from types import SimpleNamespace

import jax
import jax.numpy as jnp
from jax import lax
from jax.experimental import pallas as pl
from jax.experimental.pallas import tpu as pltpu
from jax.sharding import PartitionSpec as P

BLOCK = 128
CHUNK = 16
F32 = jnp.float32
BF16 = jnp.bfloat16
LOG2E = 1.4426950408889634
MESH = pl.DeviceIdType.MESH
OUTS = ("o", "dq", "dk", "dv")


def bit_reversed(value, bits):
    return sum(((value >> bit) & 1) << (bits - 1 - bit) for bit in range(bits))


def dot_nt(a, b):
    return lax.dot_general(a, b, (((1,), (1,)), ((), ())), preferred_element_type=F32)


def dot_nn(a, b):
    return lax.dot_general(a, b, (((1,), (0,)), ((), ())), preferred_element_type=F32)


def dot_tn(a, b):
    return lax.dot_general(a, b, (((0,), (0,)), ((), ())), preferred_element_type=F32)


def flipped(index, mask):
    for bit in range(mask.bit_length()):
        if mask >> bit & 1:
            index = index + (1 << bit) - (2 << bit) * ((index // (1 << bit)) % 2)
    return index


def twice(x):
    return jnp.concatenate([x, x], 0)


def halves_sum(x):
    n = x.shape[0] // 2
    return x[:n] + x[n:]


def run_sums(x, bits):
    n = x.shape[0]
    row = lax.broadcasted_iota(jnp.int32, x.shape, 0)
    for bit in range(bits):
        step = 1 << bit
        up, down = pltpu.roll(x, n - step, 0), pltpu.roll(x, step, 0)
        x = x + jnp.where((row & step) == 0, up, down)
    return x


def pack_columns(parts):
    lane = lax.broadcasted_iota(jnp.int32, (8, 128), 1)
    packed = parts[0]
    for k in range(1, len(parts)):
        packed = jnp.where(lane >= 16 * k, parts[k], packed)
    return packed


def unpack_columns(packed, first, count):
    return jnp.concatenate(
        [jnp.broadcast_to(packed[:, 16 * k : 16 * k + 1], (8, 128)) for k in range(first, first + count)], 0
    )


class Plan:
    def __init__(self, rows, heads, width, devices):
        self.rows, self.heads, self.width, self.devices = rows, heads, width, devices
        self.levels = (rows * devices // BLOCK).bit_length() - 1
        self.mine = heads // 2
        self.pitch = heads * CHUNK + 8
        self.offset = {}
        total = 0
        for level in range(self.levels):
            self.offset[level] = total
            total += self.kept(level)
        self.depth = total
        self.high = list(range(5, self.levels))

    def kept(self, level):
        return max(self.rows >> level, CHUNK)

    def chips(self, level):
        return 1 << (level - 2)

    def weight(self, level):
        return float(1 << min(level, 4))

    def span(self, level):
        return pl.ds(self.offset[level], self.kept(level))

    def scratch(self):
        r, m, w, d = self.rows, self.mine, self.width, self.depth
        flat = (r // CHUNK * self.pitch, w)
        two = r + r // 2
        s = SimpleNamespace()
        vm = pltpu.VMEM
        s.inn = {name: vm((r, self.heads, w), BF16) for name in "kvqg"}
        s.flat = {name: vm(flat, F32) for name in "kvqg"}
        s.k = vm((3, m, two, w), BF16)
        s.v = vm((3, m, two, w), BF16)
        s.q = vm((3, m, d, w), BF16)
        s.g = vm((3, m, r, w), BF16)
        s.st_m, s.st_l, s.st_num, s.st_d, s.st_dq = (vm((2, m, d, w), F32) for _ in range(5))
        s.p, s.snd, s.got, s.ret, s.back = {}, {}, {}, {}, {}
        s.st_g = vm((2, m, d, w), BF16)
        s.p[0] = vm((2, m, r, r), BF16)
        s.p[1] = vm((2, m, BLOCK, BLOCK), BF16)
        s.p[2] = vm((m, BLOCK, BLOCK), BF16)
        s.p[3] = vm((m, BLOCK // 2, BLOCK), BF16)
        s.p[4] = vm((BLOCK, BLOCK), BF16)
        s.dk = vm((2, m, r, w), F32)
        s.dv = vm((2, m, r, w), F32)
        s.snd[2] = vm((2, m, 2, 64, w), BF16)
        s.got[2] = vm((2, m, 2, 64, w), BF16)
        s.snd[3] = vm((2, m, 2, 32, w), BF16)
        s.got[3] = vm((2, m, 2, 32, w), BF16)
        s.der3 = vm((m, 2, 2, 32, w), BF16)
        s.far3 = vm((m, 2, 2, 32, w), BF16)
        s.snd[4] = vm((2, m, 2, 16, w), BF16)
        s.got[4] = vm((m, 2, 2, 16, w), BF16)
        s.q4 = vm((m, 2, 16, w), BF16)
        s.num4 = vm((m, 32, w), BF16)
        s.num4in = vm((m, 32, w), BF16)
        s.stat4 = vm((m, 8, w), F32)
        s.stat4in = vm((m, 8, w), F32)
        s.g4out = vm((m, 32, w), BF16)
        s.g4 = vm((m, 32, w), BF16)
        s.d4out = vm((m, 8, w), F32)
        s.d4 = vm((m, 8, w), F32)
        s.dq4 = vm((m, 32, w), BF16)
        s.dq4in = vm((m, 32, w), BF16)
        s.ret[4] = vm((m, 2, 2, 16, w), BF16)
        s.back[4] = vm((m, 2, 2, 16, w), BF16)
        s.dkv2 = vm((m, 2, 2, 64, w), F32)
        s.ret[2] = vm((m, 2, 2, 64, w), BF16)
        s.back[2] = vm((m, 2, 2, 64, w), BF16)
        s.ret[3] = vm((m, 2, 2, 2, 32, w), BF16)
        s.back[3] = vm((m, 2, 2, 2, 32, w), BF16)
        s.give, s.take = ({name: vm((m, r, w), BF16) for name in OUTS} for _ in range(2))
        for level in self.high:
            n = self.chips(level)
            s.snd[level] = vm((2, m, 2, 16, w), BF16)
            s.got[level] = vm((n, 2, m, 2, 16, w), BF16)
            s.ret[level] = vm((n, 2, m, 2, 16, w), BF16)
            s.back[level] = vm((n, 2, m, 2, 16, w), BF16)
            s.p[level] = vm((m, 32, n * 32), BF16)
        dma = pltpu.SemaphoreType.DMA
        s.sem_in = dma((4,))
        sems = [
            ("ex", (4,)), ("fin", (4, m)), ("2", (2, m)), ("3", (2,)), ("3d", (m,)), ("4", (2, m)),
            ("q4", (2, m)), ("n4", (m,)), ("t4", (m,)), ("g4", (m,)), ("d4", (m,)), ("x4", (m,)), ("b4", (m,)),
            ("b2", (m,)), ("b3", (m, 2)), ("3x", (m, 2)),
        ]
        for level in self.high:
            n = self.chips(level)
            sems += [("h" + str(level), (n, 2)), ("r" + str(level), (n,))]
        s.send, s.recv = ({name: dma(shape) for name, shape in sems} for _ in range(2))
        return vars(s)


def kernel(plan, *refs, **scratch):
    hbm_in, outs = refs[:4], refs[4:8]
    R = SimpleNamespace(**scratch)
    pitch = plan.pitch
    rows, heads, width, mine = plan.rows, plan.heads, plan.width, plan.mine
    levels, high = plan.levels, plan.high
    factor = width ** (-0.5)
    chunks = rows // CHUNK

    me = lax.axis_index("seq")
    core = me % 2
    chip = me // 2
    sibling = me + 1 - 2 * core
    place = chip % 4
    turned = [flipped(place, i) for i in range(4)]

    def device(chip_mask, other):
        return flipped(chip, chip_mask) * 2 + (1 - core if other else core)

    def remote(src, dst, name, index, peer):
        return pltpu.make_async_remote_copy(
            src_ref=src, dst_ref=dst, send_sem=R.send[name].at[index], recv_sem=R.recv[name].at[index],
            device_id={"seq": peer}, device_id_type=MESH,
        )

    def arrived(ref, name, index):
        remote(ref, ref, name, index, sibling).wait_recv()

    fetch = {
        name: pltpu.make_async_copy(ref, R.inn[name], R.sem_in.at[i])
        for i, (name, ref) in enumerate(zip("qkvg", hbm_in))
    }
    for name in "kvqg":
        fetch[name].start()

    peers = [sibling]
    for mask in range(1, 8):
        peers += [device(mask, False), device(mask, True)]
    for level in high:
        for j in range(plan.chips(level)):
            peers += [device(plan.chips(level) ^ j, False), device(plan.chips(level) ^ j, True)]
    barrier = pltpu.get_barrier_semaphore()
    for peer in peers:
        pl.semaphore_signal(barrier, inc=1, device_id={"seq": peer}, device_id_type=MESH)

    direct = (mine - 1,)
    sent = []

    def start(copy):
        copy.start()
        sent.append(copy)

    def spread(names):
        for name in names:
            fetch[name].wait()

        def body(i, carry):
            for name in names:
                x = R.inn[name][pl.ds(i * CHUNK, CHUNK)].astype(F32)
                R.flat[name][pl.ds(i * pitch, CHUNK * heads), :] = x.reshape(CHUNK * heads, width)
            return carry

        lax.fori_loop(0, chunks, body, 0)

    def head_rows(name, head):
        flat = R.flat[name]
        return jnp.concatenate(
            [flat[pl.ds(bit_reversed(b, 4) * heads + head, CHUNK, stride=pitch), :] for b in range(16)], 0
        )

    def coarse(x):
        out = [x]
        for level in range(1, levels):
            if level <= 4:
                out.append(halves_sum(out[-1]))
            else:
                out.append(run_sums(out[4], level - 4))
        return [(y * 0.5**level).astype(BF16) for level, y in enumerate(out)]

    def split_kv(hl, carry):
        for d in range(2):
            head = (core if d == 0 else 1 - core) * mine + hl
            for which, name in enumerate("kv"):
                x = coarse(head_rows(name, head))
                slot = 2 * d
                vars(R)[name][slot, hl, pl.ds(0, rows)] = x[0]
                vars(R)[name][slot, hl, pl.ds(rows, rows // 2)] = x[1]
                for level in range(2, levels):
                    R.snd[level][d, hl, which] = x[level]
        return carry

    def split_qg(hl, carry):
        for d in range(2):
            head = (core if d == 0 else 1 - core) * mine + hl
            slot = 2 * d
            for level, x in enumerate(coarse(head_rows("q", head))):
                R.q[slot, hl, plan.span(level)] = x
            R.g[slot, hl] = head_rows("g", head).astype(BF16)
        return carry

    def attend(q, k, v):
        s = dot_nt(q, k)
        m = jnp.max(s, axis=1, keepdims=True)
        p = jnp.exp2((s - m) * (factor * LOG2E))
        low = p.astype(BF16)
        num = dot_nn(low, v)
        shape = (s.shape[0], width)
        total = jnp.sum(p, axis=1, keepdims=True)
        return low, jnp.broadcast_to(m * factor, shape), jnp.broadcast_to(total, shape), num

    def pull(p, q, k, v, g, d):
        dp = dot_nt(g, v)
        lanes = dp.shape[1] // width
        wide = d if lanes == 1 else jnp.concatenate([d] * lanes, 1)
        ds = (p.astype(F32) * (dp - wide)).astype(BF16)
        return dot_nn(ds, k), dot_tn(ds, q), dot_tn(p, g)

    def keep(slot, hl, level, m, total, num):
        at = plan.span(level)
        R.st_m[slot, hl, at] = m
        R.st_l[slot, hl, at] = total
        R.st_num[slot, hl, at] = num

    near = pl.ds(0, rows)
    first = pl.ds(rows, rows // 2)

    def record(slot, hl, level, made):
        p, m, total, num = made
        R.p[level][slot, hl] = p
        keep(slot, hl, level, m, total, num)

    def attend_near(slot, hl):
        return attend(R.q[slot, hl, near], R.k[slot, hl, near], R.v[slot, hl, near])

    def attend_first(slot, hl):
        return attend(R.q[slot, hl, plan.span(1)], R.k[1 - slot, hl, first], R.v[1 - slot, hl, first])

    def in_pairs(body):
        def step(i, carry):
            body([2 * i, 2 * i + 1])
            return carry

        lax.fori_loop(0, mine // 2, step, 0)

    def own_forward(hls):
        made = [attend_near(0, hl) for hl in hls]
        for hl, x in zip(hls, made):
            record(0, hl, 0, x)

    def local_forward(hls):
        made = [(1, hl, 0, attend_near(1, hl)) for hl in hls]
        made += [(slot, hl, 1, attend_first(slot, hl)) for hl in hls for slot in range(2)]
        for x in made:
            record(*x)

    spread("kv")
    lax.fori_loop(0, mine, split_kv, 0)
    spread("qg")
    lax.fori_loop(0, mine, split_qg, 0)
    in_pairs(own_forward)

    pl.semaphore_wait(barrier, len(peers))

    def send2(hl):
        for d in range(2):
            start(remote(R.snd[2].at[d, hl], R.got[2].at[d, hl], "2", (d, hl), device(1, d)))

    send2(0)
    for i in reversed(range(4)):
        for d in range(2):
            start(remote(R.snd[4].at[d, turned[i]], R.got[4].at[i, d], "4", (d, i), device(4 ^ i, d)))
            if i or d:
                start(
                    remote(
                        R.q.at[2 * d, turned[i], plan.span(4)], R.q4.at[i, d], "q4", (d, i), device(i, d)
                    )
                )
    R.q4[0, 0] = R.q[0, turned[0], plan.span(4)]
    start(remote(R.k.at[2], R.k.at[1], "ex", 0, sibling))
    start(remote(R.v.at[2], R.v.at[1], "ex", 1, sibling))
    start(remote(R.q.at[2], R.q.at[1], "ex", 2, sibling))
    start(remote(R.g.at[2], R.g.at[1], "ex", 3, sibling))
    for d in range(2):
        start(remote(R.snd[3].at[d], R.got[3].at[d], "3", d, device(2, d)))
    for hl in range(1, mine):
        if hl in direct:
            for d in range(2):
                start(remote(R.snd[3].at[d, hl], R.far3.at[hl, d], "3x", (hl, d), device(3, d)))
        send2(hl)
    for level in high:
        for j in range(plan.chips(level)):
            for d in range(2):
                start(
                    remote(
                        R.snd[level].at[d], R.got[level].at[j, d], "h" + str(level), (j, d),
                        device(plan.chips(level) ^ j, d),
                    )
                )

    arrived(R.k.at[1], "ex", 0)
    arrived(R.v.at[1], "ex", 1)
    arrived(R.q.at[1], "ex", 2)
    in_pairs(local_forward)

    def both(ref, hl, level):
        return jnp.concatenate([ref[slot, hl, plan.span(level)] for slot in range(2)], 0)

    def keys2(hl, which):
        return jnp.concatenate([R.got[2][d, hl, which] for d in range(2)], 0)

    def keys3(hl, which):
        own = [R.got[3][d, hl, which] for d in range(2)]
        return jnp.concatenate(own + [R.far3[hl, d, which] for d in range(2)], 0)

    def keys4(which):
        return jnp.concatenate([R.got[4][i, d, which] for i in range(4) for d in range(2)], 0)

    def queries4():
        return jnp.concatenate([R.q4[i, d] for i in range(4) for d in range(2)], 0)

    def keys_high(level, hl, which):
        return jnp.concatenate(
            [R.got[level][j, d, hl, which] for j in range(plan.chips(level)) for d in range(2)], 0
        )

    def far_forward(level, hl, k, v):
        p, m, total, num = attend(both(R.q, hl, level), k, v)
        R.p[level][hl] = p
        n = plan.kept(level)
        for slot in range(2):
            at = slice(slot * n, (slot + 1) * n)
            keep(slot, hl, level, m[at], total[at], num[at])

    def step_a(hl):
        for d in range(2):
            arrived(R.got[2].at[d, hl], "2", (d, hl))
        if hl not in direct:
            for d in range(2):
                for which in range(2):
                    x = halves_sum(R.got[2][d, hl, which].astype(F32)) * 0.5
                    R.der3[hl, d, which] = x.astype(BF16)
            start(remote(R.der3.at[hl], R.far3.at[hl], "3d", hl, device(2, False)))
        far_forward(2, hl, keys2(hl, 0), keys2(hl, 1))

    def forward4():
        for i in range(4):
            for d in range(2):
                arrived(R.got[4].at[i, d], "4", (d, i))
                if i or d:
                    arrived(R.q4.at[i, d], "q4", (d, i))
        q = queries4()
        p, m, total, num = attend(q, keys4(0), keys4(1))
        R.p[4][...] = p
        for i in range(4):
            at = slice(32 * i, 32 * i + 32)
            R.num4[i] = num[at].astype(BF16)
            cut = [x[32 * i + 8 * n : 32 * i + 8 * n + 8] for x in (m, total) for n in range(4)]
            R.stat4[i] = pack_columns(cut)
        R.num4in[turned[0]] = R.num4[0]
        R.stat4in[turned[0]] = R.stat4[0]
        for i in range(1, 4):
            start(remote(R.num4.at[i], R.num4in.at[turned[0]], "n4", i, device(i, False)))
            start(remote(R.stat4.at[i], R.stat4in.at[turned[0]], "t4", i, device(i, False)))

    def take4():
        for i in range(1, 4):
            arrived(R.num4in.at[turned[i]], "n4", i)
            arrived(R.stat4in.at[turned[i]], "t4", i)

    def merge(slot, hl):
        state = None
        scales = {}
        for level in reversed(range(levels)):
            if level == 4:
                stat = R.stat4in[hl]
                m = unpack_columns(stat, 2 * slot, 2)
                total = unpack_columns(stat, 4 + 2 * slot, 2)
                num = R.num4in[hl, pl.ds(16 * slot, 16)].astype(F32)
            else:
                at = plan.span(level)
                m, total, num = (ref[slot, hl, at] for ref in (R.st_m, R.st_l, R.st_num))
            weight = plan.weight(level)
            if state is None:
                scale_a, scale_b = None, jnp.full(m.shape, weight, F32)
                state = (m, total * weight, num * weight)
            else:
                if state[0].shape[0] < m.shape[0]:
                    state = tuple(twice(x) for x in state)
                top = jnp.maximum(state[0], m)
                scale_a = jnp.exp(state[0] - top)
                scale_b = jnp.exp(m - top) * weight
                state = (top, scale_a * state[1] + scale_b * total, scale_a * state[2] + scale_b * num)
            scales[level] = (scale_a, scale_b)
        inverse = 1.0 / state[1]
        att = state[2] * inverse
        give = R.give["o"]
        if slot:
            give[hl] = att.astype(BF16)
        else:
            put_rows("g", core * mine + hl, att)
        g = R.g[slot, hl].astype(F32)
        d = jnp.broadcast_to(jnp.sum(g * att, axis=1, keepdims=True), att.shape)
        c = scales[0][1] * inverse
        at = plan.span(0)
        R.st_g[slot, hl, at] = (g * c).astype(BF16)
        R.st_d[slot, hl, at] = d * c
        scale = scales[0][0] * inverse
        up, up_d = g * scale, d * scale
        for level in range(1, levels):
            scale_a, scale_b = scales[level]
            if up.shape[0] > scale_b.shape[0]:
                up, up_d = halves_sum(up), halves_sum(up_d)
            at = plan.span(level)
            R.st_g[slot, hl, at] = (up * scale_b).astype(BF16)
            R.st_d[slot, hl, at] = up_d * scale_b
            if scale_a is not None:
                up, up_d = up * scale_a, up_d * scale_a

    def put_rows(name, head, x):
        flat = R.flat[name]
        for b in range(16):
            flat[pl.ds(bit_reversed(b, 4) * heads + head, CHUNK, stride=pitch), :] = x[
                b * CHUNK : (b + 1) * CHUNK
            ]

    def far_backward(level, hl, k, v):
        dq, dk, dv = pull(
            R.p[level][hl], both(R.q, hl, level), k, v, both(R.st_g, hl, level), both(R.st_d, hl, level)
        )
        n = plan.kept(level)
        for slot in range(2):
            R.st_dq[slot, hl, plan.span(level)] = dq[slot * n : (slot + 1) * n]
        return dk, dv

    def step_m(hl):
        if hl in direct:
            for d in range(2):
                arrived(R.far3.at[hl, d], "3x", (hl, d))
        else:
            arrived(R.far3.at[hl], "3d", hl)
        far_forward(3, hl, keys3(hl, 0), keys3(hl, 1))
        for slot in range(2):
            merge(slot, hl)

    def step_b(hl):
        grads = far_backward(3, hl, keys3(hl, 0), keys3(hl, 1))
        for which, x in enumerate(grads):
            for block in range(2):
                for slot in range(2):
                    at = 32 * (2 * block + slot)
                    R.ret[3][hl, block, slot, which] = x[at : at + 32].astype(BF16)
        for block in range(2):
            to = device(3 if block and hl in direct else 2, False)
            start(remote(R.ret[3].at[hl, block], R.back[3].at[hl, block], "b3", (hl, block), to))
        grads = far_backward(2, hl, keys2(hl, 0), keys2(hl, 1))
        for which, x in enumerate(grads):
            for slot in range(2):
                R.dkv2[hl, slot, which] = x[64 * slot : 64 * slot + 64]

    def step_c(hl):
        if hl not in direct:
            arrived(R.back[3].at[hl, 1], "b3", (hl, 1))
        for slot in range(2):
            for which in range(2):
                x = R.dkv2[hl, slot, which]
                if hl not in direct:
                    x = x + twice(R.back[3][hl, 1, slot, which].astype(F32) * 0.5)
                R.ret[2][hl, slot, which] = x.astype(BF16)
        start(remote(R.ret[2].at[hl], R.back[2].at[hl], "b2", hl, device(1, False)))

    def share4():
        for hl in range(mine):
            R.g4out[hl] = both(R.st_g, hl, 4)
            d = both(R.st_d, hl, 4)
            R.d4out[hl] = pack_columns([d[8 * n : 8 * n + 8] for n in range(4)])
        R.g4[0] = R.g4out[turned[0]]
        R.d4[0] = R.d4out[turned[0]]
        for i in range(1, 4):
            start(remote(R.g4out.at[turned[i]], R.g4.at[i], "g4", i, device(i, False)))
            start(remote(R.d4out.at[turned[i]], R.d4.at[i], "d4", i, device(i, False)))

    def backward4():
        for i in range(1, 4):
            arrived(R.g4.at[i], "g4", i)
            arrived(R.d4.at[i], "d4", i)
        q = queries4()
        g = jnp.concatenate([R.g4[i] for i in range(4)], 0)
        d = jnp.concatenate([unpack_columns(R.d4[i], 0, 4) for i in range(4)], 0)
        dq, dk, dv = pull(R.p[4][...], q, keys4(0), keys4(1), g, d)
        for i in range(4):
            R.dq4[i] = dq[32 * i : 32 * i + 32].astype(BF16)
            for which, x in enumerate((dk, dv)):
                for slot in range(2):
                    at = 32 * i + 16 * slot
                    R.ret[4][i, slot, which] = x[at : at + 16].astype(BF16)
        R.dq4in[turned[0]] = R.dq4[0]
        for i in range(1, 4):
            start(remote(R.dq4.at[i], R.dq4in.at[turned[0]], "x4", i, device(i, False)))
        for i in range(4):
            start(remote(R.ret[4].at[i], R.back[4].at[turned[0]], "b4", i, device(4 ^ i, False)))

    def high_forward():
        for level in high:
            for j in range(plan.chips(level)):
                for d in range(2):
                    arrived(R.got[level].at[j, d], "h" + str(level), (j, d))
            for hl in range(mine):
                far_forward(level, hl, keys_high(level, hl, 0), keys_high(level, hl, 1))

    def high_backward():
        for level in high:
            n = plan.chips(level)
            for hl in range(mine):
                grads = far_backward(level, hl, keys_high(level, hl, 0), keys_high(level, hl, 1))
                for which, x in enumerate(grads):
                    for j in range(n):
                        for d in range(2):
                            at = 32 * j + 16 * d
                            R.ret[level][j, d, hl, which] = x[at : at + 16].astype(BF16)
            for j in range(n):
                start(
                    remote(
                        R.ret[level].at[j], R.back[level].at[j], "r" + str(level), j, device(n ^ j, False)
                    )
                )

    def local_backward(hls):
        made = []
        for hl in hls:
            for slot in range(2):
                at = plan.span(0)
                made.append(
                    pull(
                        R.p[0][slot, hl], R.q[slot, hl, near], R.k[slot, hl, near], R.v[slot, hl, near],
                        R.st_g[slot, hl, at], R.st_d[slot, hl, at],
                    )
                )
                at = plan.span(1)
                made.append(
                    pull(
                        R.p[1][1 - slot, hl], R.q[1 - slot, hl, at], R.k[slot, hl, first], R.v[slot, hl, first],
                        R.st_g[1 - slot, hl, at], R.st_d[1 - slot, hl, at],
                    )
                )
        for hl in hls:
            for slot in range(2):
                (dq, dk, dv), (dq1, dk1, dv1) = made.pop(0), made.pop(0)
                R.st_dq[slot, hl, plan.span(0)] = dq
                R.st_dq[1 - slot, hl, plan.span(1)] = dq1
                R.dk[slot, hl] = dk + twice(dk1 * 0.5)
                R.dv[slot, hl] = dv + twice(dv1 * 0.5)

    def hand(index, name, flat, hl, slot, x):
        if slot:
            R.give[name][hl] = x.astype(BF16)
            start(remote(R.give[name].at[hl], R.take[name].at[hl], "fin", (index, hl), sibling))
        else:
            put_rows(flat, core * mine + hl, x)

    def total_q(slot, hl):
        extra = None
        for level in reversed(range(levels)):
            if level == 4:
                x = R.dq4in[hl, pl.ds(16 * slot, 16)].astype(F32)
            else:
                x = R.st_dq[slot, hl, plan.span(level)]
            if level > 4:
                x = run_sums(x, level - 4)
            x = x * 0.5**level
            if extra is None:
                extra = x
            else:
                extra = x + (extra if extra.shape[0] == x.shape[0] else twice(extra))
        return extra * factor

    def total_kv(slot, hl, which):
        extra = R.back[4][hl, slot, which].astype(F32) * 0.5**4
        for level in high:
            x = R.back[level][0, slot, hl, which].astype(F32)
            for j in range(1, plan.chips(level)):
                x = x + R.back[level][j, slot, hl, which].astype(F32)
            extra = extra + run_sums(x, level - 4) * 0.5**level
        x = R.back[3][hl, 0, slot, which].astype(F32)
        if hl in direct:
            x = x + R.back[3][hl, 1, slot, which].astype(F32)
        extra = x * 0.5**3 + twice(extra)
        extra = R.back[2][hl, slot, which].astype(F32) * 0.5**2 + twice(extra)
        x = (R.dk, R.dv)[which][slot, hl] + twice(twice(extra))
        return x if which else x * factor

    def collect(index, name, flat):
        for hl in range(mine):
            arrived(R.take[name].at[hl], "fin", (index, hl))
            put_rows(flat, (1 - core) * mine + hl, R.take[name][hl].astype(F32))

        def body(i, carry):
            x = R.flat[flat][pl.ds(i * pitch, CHUNK * heads), :]
            outs[index][pl.ds(i * CHUNK, CHUNK)] = x.reshape(CHUNK, heads, width).astype(BF16)
            return carry

        lax.fori_loop(0, chunks, body, 0)

    step_a(0)
    forward4()
    step_a(1)
    for d in range(2):
        arrived(R.got[3].at[d], "3", d)
    step_a(2)
    step_a(3)
    high_forward()
    arrived(R.g.at[1], "ex", 3)
    take4()
    step_m(0)
    step_b(0)
    step_m(1)
    step_b(1)
    step_m(2)
    step_m(3)
    share4()
    step_c(0)
    step_b(3)
    step_c(3)
    step_c(1)
    step_b(2)
    for hl in range(mine):
        start(remote(R.give["o"].at[hl], R.take["o"].at[hl], "fin", (0, hl), sibling))
    high_backward()
    backward4()
    step_c(2)
    in_pairs(local_backward)
    collect(0, "o", "g")
    for i in range(1, 4):
        arrived(R.dq4in.at[turned[i]], "x4", i)
    for hl in range(mine):
        for slot in (1, 0):
            hand(1, "dq", "q", hl, slot, total_q(slot, hl))
    collect(1, "dq", "q")
    for i in range(4):
        arrived(R.back[4].at[turned[i]], "b4", i)
    for level in high:
        for j in range(plan.chips(level)):
            arrived(R.back[level].at[j], "r" + str(level), j)
    for hl in range(mine):
        arrived(R.back[2].at[hl], "b2", hl)
        for block in range(1 + (hl in direct)):
            arrived(R.back[3].at[hl, block], "b3", (hl, block))
        for slot in (1, 0):
            for which, name in enumerate("kv"):
                hand(2 + which, "d" + name, name, hl, slot, total_kv(slot, hl, which))
    collect(2, "dk", "k")
    collect(3, "dv", "v")
    for copy in sent:
        copy.wait_send()


def hand_over(*refs):
    held, made, leave = refs[:4], refs[4:8], refs[8]
    outward = [pltpu.make_async_copy(held[i], made[i], leave.at[i]) for i in range(4)]
    for copy in outward:
        copy.start()
    for copy in outward:
        copy.wait()


def on_device(query_rows, key_rows, value_rows, out_grad):
    rows, heads, width = query_rows.shape
    plan = Plan(rows, heads, width, lax.axis_size("seq"))
    whole = pl.BlockSpec(memory_space=pl.ANY)
    vmem = pl.BlockSpec(memory_space=pltpu.VMEM)
    out = jax.ShapeDtypeStruct(query_rows.shape, BF16)
    made = pl.pallas_call(
        partial(kernel, plan),
        out_shape=(pltpu.VMEM(query_rows.shape, BF16),) * 4,
        in_specs=[whole] * 4,
        out_specs=(vmem,) * 4,
        scratch_shapes=plan.scratch(),
        compiler_params=pltpu.CompilerParams(
            collective_id=0, has_side_effects=True, vmem_limit_bytes=54 << 20
        ),
    )(query_rows, key_rows, value_rows, out_grad)
    return pl.pallas_call(
        hand_over,
        out_shape=(out, out, out, out),
        in_specs=[vmem] * 4,
        out_specs=(whole,) * 4,
        scratch_shapes=[pltpu.SemaphoreType.DMA((4,))],
    )(*[pltpu.with_memory_space_constraint(x, pltpu.VMEM) for x in made])


def solution(mesh):
    spec = P(("groups", "seq"), None, None)
    return jax.shard_map(
        on_device,
        mesh=mesh,
        in_specs=(spec,) * 4,
        out_specs=(spec,) * 4,
        check_vma=False,
    )
```

```python
from functools import partial
from types import SimpleNamespace

import jax
import jax.numpy as jnp
from jax import lax
from jax.experimental import pallas as pl
from jax.experimental.pallas import tpu as pltpu
from jax.sharding import PartitionSpec as P

BLOCK = 128
CHUNK = 16
F32 = jnp.float32
BF16 = jnp.bfloat16
LOG2E = 1.4426950408889634
MESH = pl.DeviceIdType.MESH
OUTS = ("o", "dq", "dk", "dv")


def bit_reversed(value, bits):
    return sum(((value >> bit) & 1) << (bits - 1 - bit) for bit in range(bits))


def dot_nt(a, b):
    return lax.dot_general(a, b, (((1,), (1,)), ((), ())), preferred_element_type=F32)


def dot_nn(a, b):
    return lax.dot_general(a, b, (((1,), (0,)), ((), ())), preferred_element_type=F32)


def dot_tn(a, b):
    return lax.dot_general(a, b, (((0,), (0,)), ((), ())), preferred_element_type=F32)


def flipped(index, mask):
    for bit in range(mask.bit_length()):
        if mask >> bit & 1:
            index = index + (1 << bit) - (2 << bit) * ((index // (1 << bit)) % 2)
    return index


def twice(x):
    return jnp.concatenate([x, x], 0)


def halves_sum(x):
    n = x.shape[0] // 2
    return x[:n] + x[n:]


def run_sums(x, bits):
    n = x.shape[0]
    row = lax.broadcasted_iota(jnp.int32, x.shape, 0)
    for bit in range(bits):
        step = 1 << bit
        up, down = pltpu.roll(x, n - step, 0), pltpu.roll(x, step, 0)
        x = x + jnp.where((row & step) == 0, up, down)
    return x


def pack_columns(parts):
    lane = lax.broadcasted_iota(jnp.int32, (8, 128), 1)
    packed = parts[0]
    for k in range(1, len(parts)):
        packed = jnp.where(lane >= 16 * k, parts[k], packed)
    return packed


def unpack_columns(packed, first, count):
    return jnp.concatenate(
        [jnp.broadcast_to(packed[:, 16 * k : 16 * k + 1], (8, 128)) for k in range(first, first + count)], 0
    )


class Plan:
    def __init__(self, rows, heads, width, devices):
        self.rows, self.heads, self.width, self.devices = rows, heads, width, devices
        self.levels = (rows * devices // BLOCK).bit_length() - 1
        self.mine = heads // 2
        self.pitch = heads * CHUNK + 8
        self.offset = {}
        total = 0
        for level in range(self.levels):
            self.offset[level] = total
            total += self.kept(level)
        self.depth = total
        self.high = list(range(5, self.levels))

    def kept(self, level):
        return max(self.rows >> level, CHUNK)

    def chips(self, level):
        return 1 << (level - 2)

    def weight(self, level):
        return float(1 << min(level, 4))

    def span(self, level):
        return pl.ds(self.offset[level], self.kept(level))

    def scratch(self):
        r, m, w, d = self.rows, self.mine, self.width, self.depth
        flat = (r // CHUNK * self.pitch, w)
        two = r + r // 2
        s = SimpleNamespace()
        vm = pltpu.VMEM
        s.inn = {name: vm((r, self.heads, w), BF16) for name in "kvqg"}
        s.flat = {name: vm(flat, F32) for name in "kvqg"}
        s.k = vm((3, m, two, w), BF16)
        s.v = vm((3, m, two, w), BF16)
        s.q = vm((3, m, d, w), BF16)
        s.g = vm((3, m, r, w), BF16)
        s.st_m, s.st_l, s.st_num, s.st_d, s.st_dq = (vm((2, m, d, w), F32) for _ in range(5))
        s.p, s.snd, s.got, s.ret, s.back = {}, {}, {}, {}, {}
        s.st_g = vm((2, m, d, w), BF16)
        s.p[0] = vm((2, m, r, r), BF16)
        s.p[1] = vm((2, m, BLOCK, BLOCK), BF16)
        s.p[2] = vm((m, BLOCK, BLOCK), BF16)
        s.p[3] = vm((m, BLOCK // 2, BLOCK), BF16)
        s.p[4] = vm((BLOCK, BLOCK), BF16)
        s.dk = vm((2, m, r, w), F32)
        s.dv = vm((2, m, r, w), F32)
        s.snd[2] = vm((2, m, 2, 64, w), BF16)
        s.got[2] = vm((2, m, 2, 64, w), BF16)
        s.snd[3] = vm((2, m, 2, 32, w), BF16)
        s.got[3] = vm((2, m, 2, 32, w), BF16)
        s.der3 = vm((m, 2, 2, 32, w), BF16)
        s.far3 = vm((m, 2, 2, 32, w), BF16)
        s.snd[4] = vm((2, m, 2, 16, w), BF16)
        s.got[4] = vm((m, 2, 2, 16, w), BF16)
        s.q4 = vm((m, 2, 16, w), BF16)
        s.num4 = vm((m, 32, w), BF16)
        s.num4in = vm((m, 32, w), BF16)
        s.stat4 = vm((m, 8, w), F32)
        s.stat4in = vm((m, 8, w), F32)
        s.g4out = vm((m, 32, w), BF16)
        s.g4 = vm((m, 32, w), BF16)
        s.d4out = vm((m, 8, w), F32)
        s.d4 = vm((m, 8, w), F32)
        s.dq4 = vm((m, 32, w), BF16)
        s.dq4in = vm((m, 32, w), BF16)
        s.ret[4] = vm((m, 2, 2, 16, w), BF16)
        s.back[4] = vm((m, 2, 2, 16, w), BF16)
        s.dkv2 = vm((m, 2, 2, 64, w), F32)
        s.ret[2] = vm((m, 2, 2, 64, w), BF16)
        s.back[2] = vm((m, 2, 2, 64, w), BF16)
        s.ret[3] = vm((m, 2, 2, 2, 32, w), BF16)
        s.back[3] = vm((m, 2, 2, 2, 32, w), BF16)
        s.give, s.take = ({name: vm((m, r, w), BF16) for name in OUTS} for _ in range(2))
        for level in self.high:
            n = self.chips(level)
            s.snd[level] = vm((2, m, 2, 16, w), BF16)
            s.got[level] = vm((n, 2, m, 2, 16, w), BF16)
            s.ret[level] = vm((n, 2, m, 2, 16, w), BF16)
            s.back[level] = vm((n, 2, m, 2, 16, w), BF16)
            s.p[level] = vm((m, 32, n * 32), BF16)
        dma = pltpu.SemaphoreType.DMA
        s.sem_in = dma((4,))
        sems = [
            ("ex", (4,)), ("fin", (4, m)), ("2", (2, m)), ("3", (2,)), ("3d", (m,)), ("4", (2, m)),
            ("q4", (2, m)), ("n4", (m,)), ("t4", (m,)), ("g4", (m,)), ("d4", (m,)), ("x4", (m,)), ("b4", (m,)),
            ("b2", (m,)), ("b3", (m, 2)), ("3x", (m, 2)),
        ]
        for level in self.high:
            n = self.chips(level)
            sems += [("h" + str(level), (n, 2)), ("r" + str(level), (n,))]
        s.send, s.recv = ({name: dma(shape) for name, shape in sems} for _ in range(2))
        return vars(s)


def kernel(plan, *refs, **scratch):
    hbm_in, outs = refs[:4], refs[4:8]
    R = SimpleNamespace(**scratch)
    pitch = plan.pitch
    rows, heads, width, mine = plan.rows, plan.heads, plan.width, plan.mine
    levels, high = plan.levels, plan.high
    factor = width ** (-0.5)
    chunks = rows // CHUNK

    me = lax.axis_index("seq")
    core = me % 2
    chip = me // 2
    sibling = me + 1 - 2 * core
    place = chip % 4
    turned = [flipped(place, i) for i in range(4)]

    def device(chip_mask, other):
        return flipped(chip, chip_mask) * 2 + (1 - core if other else core)

    def remote(src, dst, name, index, peer):
        return pltpu.make_async_remote_copy(
            src_ref=src, dst_ref=dst, send_sem=R.send[name].at[index], recv_sem=R.recv[name].at[index],
            device_id={"seq": peer}, device_id_type=MESH,
        )

    def arrived(ref, name, index):
        remote(ref, ref, name, index, sibling).wait_recv()

    fetch = {
        name: pltpu.make_async_copy(ref, R.inn[name], R.sem_in.at[i])
        for i, (name, ref) in enumerate(zip("qkvg", hbm_in))
    }
    for name in "kvqg":
        fetch[name].start()

    peers = [sibling]
    for mask in range(1, 8):
        peers += [device(mask, False), device(mask, True)]
    for level in high:
        for j in range(plan.chips(level)):
            peers += [device(plan.chips(level) ^ j, False), device(plan.chips(level) ^ j, True)]
    barrier = pltpu.get_barrier_semaphore()
    for peer in peers:
        pl.semaphore_signal(barrier, inc=1, device_id={"seq": peer}, device_id_type=MESH)

    direct = (mine - 1,)
    sent = []

    def start(copy):
        copy.start()
        sent.append(copy)

    def spread(names):
        for name in names:
            fetch[name].wait()

        def body(i, carry):
            for name in names:
                x = R.inn[name][pl.ds(i * CHUNK, CHUNK)].astype(F32)
                R.flat[name][pl.ds(i * pitch, CHUNK * heads), :] = x.reshape(CHUNK * heads, width)
            return carry

        lax.fori_loop(0, chunks, body, 0)

    def head_rows(name, head):
        flat = R.flat[name]
        return jnp.concatenate(
            [flat[pl.ds(bit_reversed(b, 4) * heads + head, CHUNK, stride=pitch), :] for b in range(16)], 0
        )

    def coarse(x):
        out = [x]
        for level in range(1, levels):
            if level <= 4:
                out.append(halves_sum(out[-1]))
            else:
                out.append(run_sums(out[4], level - 4))
        return [(y * 0.5**level).astype(BF16) for level, y in enumerate(out)]

    def split_kv(hl, carry):
        for d in range(2):
            head = (core if d == 0 else 1 - core) * mine + hl
            for which, name in enumerate("kv"):
                x = coarse(head_rows(name, head))
                slot = 2 * d
                vars(R)[name][slot, hl, pl.ds(0, rows)] = x[0]
                vars(R)[name][slot, hl, pl.ds(rows, rows // 2)] = x[1]
                for level in range(2, levels):
                    R.snd[level][d, hl, which] = x[level]
        return carry

    def split_qg(hl, carry):
        for d in range(2):
            head = (core if d == 0 else 1 - core) * mine + hl
            slot = 2 * d
            for level, x in enumerate(coarse(head_rows("q", head))):
                R.q[slot, hl, plan.span(level)] = x
            R.g[slot, hl] = head_rows("g", head).astype(BF16)
        return carry

    def attend(q, k, v):
        s = dot_nt(q, k)
        m = jnp.max(s, axis=1, keepdims=True)
        p = jnp.exp2((s - m) * (factor * LOG2E))
        low = p.astype(BF16)
        num = dot_nn(low, v)
        shape = (s.shape[0], width)
        total = jnp.sum(p, axis=1, keepdims=True)
        return low, jnp.broadcast_to(m * factor, shape), jnp.broadcast_to(total, shape), num

    def pull(p, q, k, v, g, d):
        dp = dot_nt(g, v)
        lanes = dp.shape[1] // width
        wide = d if lanes == 1 else jnp.concatenate([d] * lanes, 1)
        ds = (p.astype(F32) * (dp - wide)).astype(BF16)
        return dot_nn(ds, k), dot_tn(ds, q), dot_tn(p, g)

    def keep(slot, hl, level, m, total, num):
        at = plan.span(level)
        R.st_m[slot, hl, at] = m
        R.st_l[slot, hl, at] = total
        R.st_num[slot, hl, at] = num

    near = pl.ds(0, rows)
    first = pl.ds(rows, rows // 2)

    def record(slot, hl, level, made):
        p, m, total, num = made
        R.p[level][slot, hl] = p
        keep(slot, hl, level, m, total, num)

    def attend_near(slot, hl):
        return attend(R.q[slot, hl, near], R.k[slot, hl, near], R.v[slot, hl, near])

    def attend_first(slot, hl):
        return attend(R.q[slot, hl, plan.span(1)], R.k[1 - slot, hl, first], R.v[1 - slot, hl, first])

    def in_pairs(body):
        def step(i, carry):
            body([2 * i, 2 * i + 1])
            return carry

        lax.fori_loop(0, mine // 2, step, 0)

    def own_forward(hls):
        made = [attend_near(0, hl) for hl in hls]
        for hl, x in zip(hls, made):
            record(0, hl, 0, x)

    def local_forward(hls):
        made = [(1, hl, 0, attend_near(1, hl)) for hl in hls]
        made += [(slot, hl, 1, attend_first(slot, hl)) for hl in hls for slot in range(2)]
        for x in made:
            record(*x)

    spread("kv")
    lax.fori_loop(0, mine, split_kv, 0)
    spread("qg")
    lax.fori_loop(0, mine, split_qg, 0)
    in_pairs(own_forward)

    pl.semaphore_wait(barrier, len(peers))

    def send2(hl):
        for d in range(2):
            start(remote(R.snd[2].at[d, hl], R.got[2].at[d, hl], "2", (d, hl), device(1, d)))

    for i in reversed(range(4)):
        for d in range(2):
            start(remote(R.snd[4].at[d, turned[i]], R.got[4].at[i, d], "4", (d, i), device(4 ^ i, d)))
            if i or d:
                start(
                    remote(
                        R.q.at[2 * d, turned[i], plan.span(4)], R.q4.at[i, d], "q4", (d, i), device(i, d)
                    )
                )
    R.q4[0, 0] = R.q[0, turned[0], plan.span(4)]
    send2(0)
    start(remote(R.k.at[2], R.k.at[1], "ex", 0, sibling))
    start(remote(R.v.at[2], R.v.at[1], "ex", 1, sibling))
    start(remote(R.q.at[2], R.q.at[1], "ex", 2, sibling))
    start(remote(R.g.at[2], R.g.at[1], "ex", 3, sibling))
    for d in range(2):
        start(remote(R.snd[3].at[d], R.got[3].at[d], "3", d, device(2, d)))
    for hl in range(mine):
        if hl in direct:
            for d in range(2):
                start(remote(R.snd[3].at[d, hl], R.far3.at[hl, d], "3x", (hl, d), device(3, d)))
        if hl:
            send2(hl)
    for level in high:
        for j in range(plan.chips(level)):
            for d in range(2):
                start(
                    remote(
                        R.snd[level].at[d], R.got[level].at[j, d], "h" + str(level), (j, d),
                        device(plan.chips(level) ^ j, d),
                    )
                )

    arrived(R.k.at[1], "ex", 0)
    arrived(R.v.at[1], "ex", 1)
    arrived(R.q.at[1], "ex", 2)
    def both(ref, hl, level):
        return jnp.concatenate([ref[slot, hl, plan.span(level)] for slot in range(2)], 0)

    def keys2(hl, which):
        return jnp.concatenate([R.got[2][d, hl, which] for d in range(2)], 0)

    def keys3(hl, which):
        own = [R.got[3][d, hl, which] for d in range(2)]
        return jnp.concatenate(own + [R.far3[hl, d, which] for d in range(2)], 0)

    def keys4(which):
        return jnp.concatenate([R.got[4][i, d, which] for i in range(4) for d in range(2)], 0)

    def queries4():
        return jnp.concatenate([R.q4[i, d] for i in range(4) for d in range(2)], 0)

    def keys_high(level, hl, which):
        return jnp.concatenate(
            [R.got[level][j, d, hl, which] for j in range(plan.chips(level)) for d in range(2)], 0
        )

    def far_forward(level, hl, k, v):
        p, m, total, num = attend(both(R.q, hl, level), k, v)
        R.p[level][hl] = p
        n = plan.kept(level)
        for slot in range(2):
            at = slice(slot * n, (slot + 1) * n)
            keep(slot, hl, level, m[at], total[at], num[at])

    def derive(hl):
        for d in range(2):
            arrived(R.got[2].at[d, hl], "2", (d, hl))
        if hl not in direct:
            for d in range(2):
                for which in range(2):
                    x = halves_sum(R.got[2][d, hl, which].astype(F32)) * 0.5
                    R.der3[hl, d, which] = x.astype(BF16)
            start(remote(R.der3.at[hl], R.far3.at[hl], "3d", hl, device(2, False)))

    def step_a(hl):
        far_forward(2, hl, keys2(hl, 0), keys2(hl, 1))

    def forward4():
        for i in range(4):
            for d in range(2):
                arrived(R.got[4].at[i, d], "4", (d, i))
                if i or d:
                    arrived(R.q4.at[i, d], "q4", (d, i))
        q = queries4()
        p, m, total, num = attend(q, keys4(0), keys4(1))
        R.p[4][...] = p
        for i in range(4):
            at = slice(32 * i, 32 * i + 32)
            R.num4[i] = num[at].astype(BF16)
            cut = [x[32 * i + 8 * n : 32 * i + 8 * n + 8] for x in (m, total) for n in range(4)]
            R.stat4[i] = pack_columns(cut)
        R.num4in[turned[0]] = R.num4[0]
        R.stat4in[turned[0]] = R.stat4[0]
        for i in range(1, 4):
            start(remote(R.num4.at[i], R.num4in.at[turned[0]], "n4", i, device(i, False)))
            start(remote(R.stat4.at[i], R.stat4in.at[turned[0]], "t4", i, device(i, False)))

    def take4():
        for i in range(1, 4):
            arrived(R.num4in.at[turned[i]], "n4", i)
            arrived(R.stat4in.at[turned[i]], "t4", i)

    def merge(slot, hl):
        state = None
        scales = {}
        for level in reversed(range(levels)):
            if level == 4:
                stat = R.stat4in[hl]
                m = unpack_columns(stat, 2 * slot, 2)
                total = unpack_columns(stat, 4 + 2 * slot, 2)
                num = R.num4in[hl, pl.ds(16 * slot, 16)].astype(F32)
            else:
                at = plan.span(level)
                m, total, num = (ref[slot, hl, at] for ref in (R.st_m, R.st_l, R.st_num))
            weight = plan.weight(level)
            if state is None:
                scale_a, scale_b = None, jnp.full(m.shape, weight, F32)
                state = (m, total * weight, num * weight)
            else:
                if state[0].shape[0] < m.shape[0]:
                    state = tuple(twice(x) for x in state)
                top = jnp.maximum(state[0], m)
                scale_a = jnp.exp(state[0] - top)
                scale_b = jnp.exp(m - top) * weight
                state = (top, scale_a * state[1] + scale_b * total, scale_a * state[2] + scale_b * num)
            scales[level] = (scale_a, scale_b)
        inverse = 1.0 / state[1]
        att = state[2] * inverse
        give = R.give["o"]
        if slot:
            give[hl] = att.astype(BF16)
        else:
            put_rows("g", core * mine + hl, att)
        g = R.g[slot, hl].astype(F32)
        d = jnp.broadcast_to(jnp.sum(g * att, axis=1, keepdims=True), att.shape)
        c = scales[0][1] * inverse
        at = plan.span(0)
        R.st_g[slot, hl, at] = (g * c).astype(BF16)
        R.st_d[slot, hl, at] = d * c
        scale = scales[0][0] * inverse
        up, up_d = g * scale, d * scale
        for level in range(1, levels):
            scale_a, scale_b = scales[level]
            if up.shape[0] > scale_b.shape[0]:
                up, up_d = halves_sum(up), halves_sum(up_d)
            at = plan.span(level)
            R.st_g[slot, hl, at] = (up * scale_b).astype(BF16)
            R.st_d[slot, hl, at] = up_d * scale_b
            if scale_a is not None:
                up, up_d = up * scale_a, up_d * scale_a

    def put_rows(name, head, x):
        flat = R.flat[name]
        for b in range(16):
            flat[pl.ds(bit_reversed(b, 4) * heads + head, CHUNK, stride=pitch), :] = x[
                b * CHUNK : (b + 1) * CHUNK
            ]

    def far_backward(level, hl, k, v):
        dq, dk, dv = pull(
            R.p[level][hl], both(R.q, hl, level), k, v, both(R.st_g, hl, level), both(R.st_d, hl, level)
        )
        n = plan.kept(level)
        for slot in range(2):
            R.st_dq[slot, hl, plan.span(level)] = dq[slot * n : (slot + 1) * n]
        return dk, dv

    def step_f(hl):
        if hl in direct:
            for d in range(2):
                arrived(R.far3.at[hl, d], "3x", (hl, d))
        else:
            arrived(R.far3.at[hl], "3d", hl)
        far_forward(3, hl, keys3(hl, 0), keys3(hl, 1))

    def step_m(hl):
        for slot in range(2):
            merge(slot, hl)

    def step_b(hl):
        grads = far_backward(3, hl, keys3(hl, 0), keys3(hl, 1))
        for which, x in enumerate(grads):
            for block in range(2):
                for slot in range(2):
                    at = 32 * (2 * block + slot)
                    R.ret[3][hl, block, slot, which] = x[at : at + 32].astype(BF16)
        for block in range(2):
            to = device(3 if block and hl in direct else 2, False)
            start(remote(R.ret[3].at[hl, block], R.back[3].at[hl, block], "b3", (hl, block), to))
        grads = far_backward(2, hl, keys2(hl, 0), keys2(hl, 1))
        for which, x in enumerate(grads):
            for slot in range(2):
                R.dkv2[hl, slot, which] = x[64 * slot : 64 * slot + 64]

    def step_c(hl):
        if hl not in direct:
            arrived(R.back[3].at[hl, 1], "b3", (hl, 1))
        for slot in range(2):
            for which in range(2):
                x = R.dkv2[hl, slot, which]
                if hl not in direct:
                    x = x + twice(R.back[3][hl, 1, slot, which].astype(F32) * 0.5)
                R.ret[2][hl, slot, which] = x.astype(BF16)
        start(remote(R.ret[2].at[hl], R.back[2].at[hl], "b2", hl, device(1, False)))

    def share4():
        for hl in range(mine):
            R.g4out[hl] = both(R.st_g, hl, 4)
            d = both(R.st_d, hl, 4)
            R.d4out[hl] = pack_columns([d[8 * n : 8 * n + 8] for n in range(4)])
        R.g4[0] = R.g4out[turned[0]]
        R.d4[0] = R.d4out[turned[0]]
        for i in range(1, 4):
            start(remote(R.g4out.at[turned[i]], R.g4.at[i], "g4", i, device(i, False)))
            start(remote(R.d4out.at[turned[i]], R.d4.at[i], "d4", i, device(i, False)))

    def backward4():
        for i in range(1, 4):
            arrived(R.g4.at[i], "g4", i)
            arrived(R.d4.at[i], "d4", i)
        q = queries4()
        g = jnp.concatenate([R.g4[i] for i in range(4)], 0)
        d = jnp.concatenate([unpack_columns(R.d4[i], 0, 4) for i in range(4)], 0)
        dq, dk, dv = pull(R.p[4][...], q, keys4(0), keys4(1), g, d)
        for i in range(4):
            R.dq4[i] = dq[32 * i : 32 * i + 32].astype(BF16)
            for which, x in enumerate((dk, dv)):
                for slot in range(2):
                    at = 32 * i + 16 * slot
                    R.ret[4][i, slot, which] = x[at : at + 16].astype(BF16)
        R.dq4in[turned[0]] = R.dq4[0]
        for i in range(1, 4):
            start(remote(R.dq4.at[i], R.dq4in.at[turned[0]], "x4", i, device(i, False)))
        for i in range(4):
            start(remote(R.ret[4].at[i], R.back[4].at[turned[0]], "b4", i, device(4 ^ i, False)))

    def high_forward():
        for level in high:
            for j in range(plan.chips(level)):
                for d in range(2):
                    arrived(R.got[level].at[j, d], "h" + str(level), (j, d))
            for hl in range(mine):
                far_forward(level, hl, keys_high(level, hl, 0), keys_high(level, hl, 1))

    def high_backward():
        for level in high:
            n = plan.chips(level)
            for hl in range(mine):
                grads = far_backward(level, hl, keys_high(level, hl, 0), keys_high(level, hl, 1))
                for which, x in enumerate(grads):
                    for j in range(n):
                        for d in range(2):
                            at = 32 * j + 16 * d
                            R.ret[level][j, d, hl, which] = x[at : at + 16].astype(BF16)
            for j in range(n):
                start(
                    remote(
                        R.ret[level].at[j], R.back[level].at[j], "r" + str(level), j, device(n ^ j, False)
                    )
                )

    def local_backward(hls):
        made = []
        for hl in hls:
            for slot in range(2):
                at = plan.span(0)
                made.append(
                    pull(
                        R.p[0][slot, hl], R.q[slot, hl, near], R.k[slot, hl, near], R.v[slot, hl, near],
                        R.st_g[slot, hl, at], R.st_d[slot, hl, at],
                    )
                )
                at = plan.span(1)
                made.append(
                    pull(
                        R.p[1][1 - slot, hl], R.q[1 - slot, hl, at], R.k[slot, hl, first], R.v[slot, hl, first],
                        R.st_g[1 - slot, hl, at], R.st_d[1 - slot, hl, at],
                    )
                )
        for hl in hls:
            for slot in range(2):
                (dq, dk, dv), (dq1, dk1, dv1) = made.pop(0), made.pop(0)
                R.st_dq[slot, hl, plan.span(0)] = dq
                R.st_dq[1 - slot, hl, plan.span(1)] = dq1
                R.dk[slot, hl] = dk + twice(dk1 * 0.5)
                R.dv[slot, hl] = dv + twice(dv1 * 0.5)

    def hand(index, name, flat, hl, slot, x):
        if slot:
            R.give[name][hl] = x.astype(BF16)
            start(remote(R.give[name].at[hl], R.take[name].at[hl], "fin", (index, hl), sibling))
        else:
            put_rows(flat, core * mine + hl, x)

    def total_q(slot, hl):
        extra = None
        for level in reversed(range(levels)):
            if level == 4:
                x = R.dq4in[hl, pl.ds(16 * slot, 16)].astype(F32)
            else:
                x = R.st_dq[slot, hl, plan.span(level)]
            if level > 4:
                x = run_sums(x, level - 4)
            x = x * 0.5**level
            if extra is None:
                extra = x
            else:
                extra = x + (extra if extra.shape[0] == x.shape[0] else twice(extra))
        return extra * factor

    def total_kv(slot, hl, which):
        extra = R.back[4][hl, slot, which].astype(F32) * 0.5**4
        for level in high:
            x = R.back[level][0, slot, hl, which].astype(F32)
            for j in range(1, plan.chips(level)):
                x = x + R.back[level][j, slot, hl, which].astype(F32)
            extra = extra + run_sums(x, level - 4) * 0.5**level
        x = R.back[3][hl, 0, slot, which].astype(F32)
        if hl in direct:
            x = x + R.back[3][hl, 1, slot, which].astype(F32)
        extra = x * 0.5**3 + twice(extra)
        extra = R.back[2][hl, slot, which].astype(F32) * 0.5**2 + twice(extra)
        x = (R.dk, R.dv)[which][slot, hl] + twice(twice(extra))
        return x if which else x * factor

    def collect(index, name, flat):
        for hl in range(mine):
            arrived(R.take[name].at[hl], "fin", (index, hl))
            put_rows(flat, (1 - core) * mine + hl, R.take[name][hl].astype(F32))

        def body(i, carry):
            x = R.flat[flat][pl.ds(i * pitch, CHUNK * heads), :]
            outs[index][pl.ds(i * CHUNK, CHUNK)] = x.reshape(CHUNK, heads, width).astype(BF16)
            return carry

        lax.fori_loop(0, chunks, body, 0)

    in_pairs(local_forward)
    derive(0)
    step_a(0)
    forward4()
    derive(1)
    step_a(1)
    for d in range(2):
        arrived(R.got[3].at[d], "3", d)
    derive(2)
    step_a(2)
    derive(3)
    step_a(3)
    high_forward()
    arrived(R.g.at[1], "ex", 3)
    take4()
    step_f(0)
    step_m(0)
    step_b(0)
    step_f(1)
    step_m(1)
    step_b(1)
    step_f(2)
    step_m(2)
    step_f(3)
    step_m(3)
    share4()
    step_c(0)
    step_b(3)
    step_c(3)
    step_c(1)
    step_b(2)
    for hl in range(mine):
        start(remote(R.give["o"].at[hl], R.take["o"].at[hl], "fin", (0, hl), sibling))
    high_backward()
    backward4()
    step_c(2)
    in_pairs(local_backward)
    for i in range(1, 4):
        arrived(R.dq4in.at[turned[i]], "x4", i)
    for hl in range(mine):
        hand(1, "dq", "q", hl, 1, total_q(1, hl))
    for i in range(4):
        arrived(R.back[4].at[turned[i]], "b4", i)
    for level in high:
        for j in range(plan.chips(level)):
            arrived(R.back[level].at[j], "r" + str(level), j)
    for hl in range(mine):
        arrived(R.back[2].at[hl], "b2", hl)
        for block in range(2):
            if block == 0 or hl in direct:
                arrived(R.back[3].at[hl, block], "b3", (hl, block))
        for which, name in enumerate("kv"):
            hand(2 + which, "d" + name, name, hl, 1, total_kv(1, hl, which))
    for hl in range(mine):
        hand(1, "dq", "q", hl, 0, total_q(0, hl))
        for which, name in enumerate("kv"):
            hand(2 + which, "d" + name, name, hl, 0, total_kv(0, hl, which))
    collect(0, "o", "g")
    collect(1, "dq", "q")
    collect(2, "dk", "k")
    collect(3, "dv", "v")
    for copy in sent:
        copy.wait_send()


def hand_over(*refs):
    held, made, leave = refs[:4], refs[4:8], refs[8]
    outward = [pltpu.make_async_copy(held[i], made[i], leave.at[i]) for i in range(4)]
    for copy in outward:
        copy.start()
    for copy in outward:
        copy.wait()


def on_device(query_rows, key_rows, value_rows, out_grad):
    rows, heads, width = query_rows.shape
    plan = Plan(rows, heads, width, lax.axis_size("seq"))
    whole = pl.BlockSpec(memory_space=pl.ANY)
    vmem = pl.BlockSpec(memory_space=pltpu.VMEM)
    out = jax.ShapeDtypeStruct(query_rows.shape, BF16)
    made = pl.pallas_call(
        partial(kernel, plan),
        out_shape=(pltpu.VMEM(query_rows.shape, BF16),) * 4,
        in_specs=[whole] * 4,
        out_specs=(vmem,) * 4,
        scratch_shapes=plan.scratch(),
        compiler_params=pltpu.CompilerParams(
            collective_id=0, has_side_effects=True, vmem_limit_bytes=54 << 20
        ),
    )(query_rows, key_rows, value_rows, out_grad)
    return pl.pallas_call(
        hand_over,
        out_shape=(out, out, out, out),
        in_specs=[vmem] * 4,
        out_specs=(whole,) * 4,
        scratch_shapes=[pltpu.SemaphoreType.DMA((4,))],
    )(*[pltpu.with_memory_space_constraint(x, pltpu.VMEM) for x in made])


def solution(mesh):
    spec = P(("groups", "seq"), None, None)
    return jax.shard_map(
        on_device,
        mesh=mesh,
        in_specs=(spec,) * 4,
        out_specs=(spec,) * 4,
        check_vma=False,
    )
```

```python
from functools import partial
from types import SimpleNamespace

import jax
import jax.numpy as jnp
from jax import lax
from jax.experimental import pallas as pl
from jax.experimental.pallas import tpu as pltpu
from jax.sharding import PartitionSpec as P

BLOCK = 128
CHUNK = 16
F32 = jnp.float32
BF16 = jnp.bfloat16
LOG2E = 1.4426950408889634
MESH = pl.DeviceIdType.MESH
OUTS = ("o", "dq", "dk", "dv")


def bit_reversed(value, bits):
    return sum(((value >> bit) & 1) << (bits - 1 - bit) for bit in range(bits))


def dot_nt(a, b):
    return lax.dot_general(a, b, (((1,), (1,)), ((), ())), preferred_element_type=F32)


def dot_nn(a, b):
    return lax.dot_general(a, b, (((1,), (0,)), ((), ())), preferred_element_type=F32)


def dot_tn(a, b):
    return lax.dot_general(a, b, (((0,), (0,)), ((), ())), preferred_element_type=F32)


def flipped(index, mask):
    for bit in range(mask.bit_length()):
        if mask >> bit & 1:
            index = index + (1 << bit) - (2 << bit) * ((index // (1 << bit)) % 2)
    return index


def twice(x):
    return jnp.concatenate([x, x], 0)


def halves_sum(x):
    n = x.shape[0] // 2
    return x[:n] + x[n:]


def run_sums(x, bits):
    n = x.shape[0]
    row = lax.broadcasted_iota(jnp.int32, x.shape, 0)
    for bit in range(bits):
        step = 1 << bit
        up, down = pltpu.roll(x, n - step, 0), pltpu.roll(x, step, 0)
        x = x + jnp.where((row & step) == 0, up, down)
    return x


def pack_columns(parts):
    lane = lax.broadcasted_iota(jnp.int32, (8, 128), 1)
    packed = parts[0]
    for k in range(1, len(parts)):
        packed = jnp.where(lane >= 16 * k, parts[k], packed)
    return packed


def unpack_columns(packed, first, count):
    return jnp.concatenate(
        [jnp.broadcast_to(packed[:, 16 * k : 16 * k + 1], (8, 128)) for k in range(first, first + count)], 0
    )


class Plan:
    def __init__(self, rows, heads, width, devices):
        self.rows, self.heads, self.width, self.devices = rows, heads, width, devices
        self.levels = (rows * devices // BLOCK).bit_length() - 1
        self.mine = heads // 2
        self.pitch = heads * CHUNK + 8
        self.offset = {}
        total = 0
        for level in range(self.levels):
            self.offset[level] = total
            total += self.kept(level)
        self.depth = total
        self.high = list(range(5, self.levels))

    def kept(self, level):
        return max(self.rows >> level, CHUNK)

    def chips(self, level):
        return 1 << (level - 2)

    def weight(self, level):
        return float(1 << min(level, 4))

    def span(self, level):
        return pl.ds(self.offset[level], self.kept(level))

    def scratch(self):
        r, m, w, d = self.rows, self.mine, self.width, self.depth
        flat = (r // CHUNK * self.pitch, w)
        two = r + r // 2
        s = SimpleNamespace()
        vm = pltpu.VMEM
        s.inn = {name: vm((r, self.heads, w), BF16) for name in "kvqg"}
        s.flat = {name: vm(flat, F32) for name in "kvqg"}
        s.k = vm((3, m, two, w), BF16)
        s.v = vm((3, m, two, w), BF16)
        s.q = vm((3, m, d, w), BF16)
        s.g = vm((3, m, r, w), BF16)
        s.st_m, s.st_l, s.st_num, s.st_d, s.st_dq = (vm((2, m, d, w), F32) for _ in range(5))
        s.p, s.snd, s.got, s.ret, s.back = {}, {}, {}, {}, {}
        s.st_g = vm((2, m, d, w), BF16)
        s.p[0] = vm((2, m, r, r), BF16)
        s.p[1] = vm((2, m, BLOCK, BLOCK), BF16)
        s.p[2] = vm((m, BLOCK, BLOCK), BF16)
        s.p[3] = vm((m, BLOCK // 2, BLOCK), BF16)
        s.p[4] = vm((BLOCK, BLOCK), BF16)
        s.dk = vm((2, m, r, w), F32)
        s.dv = vm((2, m, r, w), F32)
        s.snd[2] = vm((2, m, 2, 64, w), BF16)
        s.got[2] = vm((2, m, 2, 64, w), BF16)
        s.snd[3] = vm((2, m, 2, 32, w), BF16)
        s.got[3] = vm((2, m, 2, 32, w), BF16)
        s.der3 = vm((m, 2, 2, 32, w), BF16)
        s.far3 = vm((m, 2, 2, 32, w), BF16)
        s.snd[4] = vm((2, m, 2, 16, w), BF16)
        s.got[4] = vm((m, 2, 2, 16, w), BF16)
        s.q4 = vm((m, 2, 16, w), BF16)
        s.num4 = vm((m, 32, w), BF16)
        s.num4in = vm((m, 32, w), BF16)
        s.stat4 = vm((m, 8, w), F32)
        s.stat4in = vm((m, 8, w), F32)
        s.g4out = vm((m, 32, w), BF16)
        s.g4 = vm((m, 32, w), BF16)
        s.d4out = vm((m, 8, w), F32)
        s.d4 = vm((m, 8, w), F32)
        s.dq4 = vm((m, 32, w), BF16)
        s.dq4in = vm((m, 32, w), BF16)
        s.ret[4] = vm((m, 2, 2, 16, w), BF16)
        s.back[4] = vm((m, 2, 2, 16, w), BF16)
        s.dkv2 = vm((m, 2, 2, 64, w), F32)
        s.ret[2] = vm((m, 2, 2, 64, w), BF16)
        s.back[2] = vm((m, 2, 2, 64, w), BF16)
        s.ret[3] = vm((m, 2, 2, 2, 32, w), BF16)
        s.back[3] = vm((m, 2, 2, 2, 32, w), BF16)
        s.give, s.take = ({name: vm((m, r, w), BF16) for name in OUTS} for _ in range(2))
        for level in self.high:
            n = self.chips(level)
            s.snd[level] = vm((2, m, 2, 16, w), BF16)
            s.got[level] = vm((n, 2, m, 2, 16, w), BF16)
            s.ret[level] = vm((n, 2, m, 2, 16, w), BF16)
            s.back[level] = vm((n, 2, m, 2, 16, w), BF16)
            s.p[level] = vm((m, 32, n * 32), BF16)
        dma = pltpu.SemaphoreType.DMA
        s.sem_in = dma((4,))
        sems = [
            ("ex", (4,)), ("fin", (4, m)), ("2", (2, m)), ("3", (2,)), ("3d", (m,)), ("4", (2, m)),
            ("q4", (2, m)), ("n4", (m,)), ("t4", (m,)), ("g4", (m,)), ("d4", (m,)), ("x4", (m,)), ("b4", (m,)),
            ("b2", (m,)), ("b3", (m, 2)), ("3x", (m, 2)),
        ]
        for level in self.high:
            n = self.chips(level)
            sems += [("h" + str(level), (n, 2)), ("r" + str(level), (n,))]
        s.send, s.recv = ({name: dma(shape) for name, shape in sems} for _ in range(2))
        return vars(s)


def kernel(plan, *refs, **scratch):
    hbm_in, outs = refs[:4], refs[4:8]
    R = SimpleNamespace(**scratch)
    pitch = plan.pitch
    rows, heads, width, mine = plan.rows, plan.heads, plan.width, plan.mine
    levels, high = plan.levels, plan.high
    factor = width ** (-0.5)
    chunks = rows // CHUNK

    me = lax.axis_index("seq")
    core = me % 2
    chip = me // 2
    sibling = me + 1 - 2 * core
    place = chip % 4
    turned = [flipped(place, i) for i in range(4)]

    def device(chip_mask, other):
        return flipped(chip, chip_mask) * 2 + (1 - core if other else core)

    def remote(src, dst, name, index, peer):
        return pltpu.make_async_remote_copy(
            src_ref=src, dst_ref=dst, send_sem=R.send[name].at[index], recv_sem=R.recv[name].at[index],
            device_id={"seq": peer}, device_id_type=MESH,
        )

    def arrived(ref, name, index):
        remote(ref, ref, name, index, sibling).wait_recv()

    fetch = {
        name: pltpu.make_async_copy(ref, R.inn[name], R.sem_in.at[i])
        for i, (name, ref) in enumerate(zip("qkvg", hbm_in))
    }
    for name in "kvqg":
        fetch[name].start()

    peers = [sibling]
    for mask in range(1, 8):
        peers += [device(mask, False), device(mask, True)]
    for level in high:
        for j in range(plan.chips(level)):
            peers += [device(plan.chips(level) ^ j, False), device(plan.chips(level) ^ j, True)]
    barrier = pltpu.get_barrier_semaphore()
    for peer in peers:
        pl.semaphore_signal(barrier, inc=1, device_id={"seq": peer}, device_id_type=MESH)

    direct = (mine - 1,)
    straight = (0, 1, 2, 3)
    sent = []

    def start(copy):
        copy.start()
        sent.append(copy)

    def spread(names):
        for name in names:
            fetch[name].wait()

        def body(i, carry):
            for name in names:
                x = R.inn[name][pl.ds(i * CHUNK, CHUNK)].astype(F32)
                R.flat[name][pl.ds(i * pitch, CHUNK * heads), :] = x.reshape(CHUNK * heads, width)
            return carry

        lax.fori_loop(0, chunks, body, 0)

    def head_rows(name, head):
        flat = R.flat[name]
        return jnp.concatenate(
            [flat[pl.ds(bit_reversed(b, 4) * heads + head, CHUNK, stride=pitch), :] for b in range(16)], 0
        )

    def coarse(x):
        out = [x]
        for level in range(1, levels):
            if level <= 4:
                out.append(halves_sum(out[-1]))
            else:
                out.append(run_sums(out[4], level - 4))
        return [(y * 0.5**level).astype(BF16) for level, y in enumerate(out)]

    def split_kv(hl, carry):
        for d in range(2):
            head = (core if d == 0 else 1 - core) * mine + hl
            for which, name in enumerate("kv"):
                x = coarse(head_rows(name, head))
                slot = 2 * d
                vars(R)[name][slot, hl, pl.ds(0, rows)] = x[0]
                vars(R)[name][slot, hl, pl.ds(rows, rows // 2)] = x[1]
                for level in range(2, levels):
                    R.snd[level][d, hl, which] = x[level]
        return carry

    def split_qg(hl, carry):
        for d in range(2):
            head = (core if d == 0 else 1 - core) * mine + hl
            slot = 2 * d
            for level, x in enumerate(coarse(head_rows("q", head))):
                R.q[slot, hl, plan.span(level)] = x
            R.g[slot, hl] = head_rows("g", head).astype(BF16)
        return carry

    def attend(q, k, v):
        s = dot_nt(q, k)
        m = jnp.max(s, axis=1, keepdims=True)
        p = jnp.exp2((s - m) * (factor * LOG2E))
        low = p.astype(BF16)
        both_sums = dot_nn(low, jnp.concatenate([v, jnp.ones(v.shape, BF16)], 1))
        m = jnp.broadcast_to(m * factor, (s.shape[0], width))
        return low, m, both_sums[:, width:], both_sums[:, :width]

    def pull(p, q, k, v, g, d):
        dp = dot_nt(g, v)
        lanes = dp.shape[1] // width
        wide = d if lanes == 1 else jnp.concatenate([d] * lanes, 1)
        ds = p * (dp - wide).astype(BF16)
        return dot_nn(ds, k), dot_tn(ds, q), dot_tn(p, g)

    def keep(slot, hl, level, m, total, num):
        at = plan.span(level)
        R.st_m[slot, hl, at] = m
        R.st_l[slot, hl, at] = total
        R.st_num[slot, hl, at] = num

    near = pl.ds(0, rows)
    first = pl.ds(rows, rows // 2)

    def record(slot, hl, level, made):
        p, m, total, num = made
        R.p[level][slot, hl] = p
        keep(slot, hl, level, m, total, num)

    def attend_near(slot, hl):
        return attend(R.q[slot, hl, near], R.k[slot, hl, near], R.v[slot, hl, near])

    def attend_first(slot, hl):
        return attend(R.q[slot, hl, plan.span(1)], R.k[1 - slot, hl, first], R.v[1 - slot, hl, first])

    def in_pairs(body):
        def step(i, carry):
            body([2 * i, 2 * i + 1])
            return carry

        lax.fori_loop(0, mine // 2, step, 0)

    def own_forward(hls):
        made = [attend_near(0, hl) for hl in hls]
        for hl, x in zip(hls, made):
            record(0, hl, 0, x)

    def local_forward(hls):
        made = [(1, hl, 0, attend_near(1, hl)) for hl in hls]
        made += [(slot, hl, 1, attend_first(slot, hl)) for hl in hls for slot in range(2)]
        for x in made:
            record(*x)

    spread("kv")
    lax.fori_loop(0, mine, split_kv, 0)
    spread("qg")
    lax.fori_loop(0, mine, split_qg, 0)
    in_pairs(own_forward)

    pl.semaphore_wait(barrier, len(peers))

    def send2(hl):
        for d in range(2):
            start(remote(R.snd[2].at[d, hl], R.got[2].at[d, hl], "2", (d, hl), device(1, d)))

    for i in reversed(range(4)):
        for d in range(2):
            start(remote(R.snd[4].at[d, turned[i]], R.got[4].at[i, d], "4", (d, i), device(4 ^ i, d)))
            if i or d:
                start(
                    remote(
                        R.q.at[2 * d, turned[i], plan.span(4)], R.q4.at[i, d], "q4", (d, i), device(i, d)
                    )
                )
    R.q4[0, 0] = R.q[0, turned[0], plan.span(4)]
    send2(0)
    start(remote(R.k.at[2], R.k.at[1], "ex", 0, sibling))
    start(remote(R.v.at[2], R.v.at[1], "ex", 1, sibling))
    start(remote(R.q.at[2], R.q.at[1], "ex", 2, sibling))
    start(remote(R.g.at[2], R.g.at[1], "ex", 3, sibling))
    for d in range(2):
        start(remote(R.snd[3].at[d], R.got[3].at[d], "3", d, device(2, d)))
    for hl in range(mine):
        if hl in direct:
            for d in range(2):
                start(remote(R.snd[3].at[d, hl], R.far3.at[hl, d], "3x", (hl, d), device(3, d)))
        if hl:
            send2(hl)
    for level in high:
        for j in range(plan.chips(level)):
            for d in range(2):
                start(
                    remote(
                        R.snd[level].at[d], R.got[level].at[j, d], "h" + str(level), (j, d),
                        device(plan.chips(level) ^ j, d),
                    )
                )

    arrived(R.k.at[1], "ex", 0)
    arrived(R.v.at[1], "ex", 1)
    arrived(R.q.at[1], "ex", 2)
    def both(ref, hl, level):
        return jnp.concatenate([ref[slot, hl, plan.span(level)] for slot in range(2)], 0)

    def keys2(hl, which):
        return jnp.concatenate([R.got[2][d, hl, which] for d in range(2)], 0)

    def keys3(hl, which):
        own = [R.got[3][d, hl, which] for d in range(2)]
        return jnp.concatenate(own + [R.far3[hl, d, which] for d in range(2)], 0)

    def keys4(which):
        return jnp.concatenate([R.got[4][i, d, which] for i in range(4) for d in range(2)], 0)

    def queries4():
        return jnp.concatenate([R.q4[i, d] for i in range(4) for d in range(2)], 0)

    def keys_high(level, hl, which):
        return jnp.concatenate(
            [R.got[level][j, d, hl, which] for j in range(plan.chips(level)) for d in range(2)], 0
        )

    def far_forward(level, hl, k, v):
        p, m, total, num = attend(both(R.q, hl, level), k, v)
        R.p[level][hl] = p
        n = plan.kept(level)
        for slot in range(2):
            at = slice(slot * n, (slot + 1) * n)
            keep(slot, hl, level, m[at], total[at], num[at])

    def derive(hl):
        for d in range(2):
            arrived(R.got[2].at[d, hl], "2", (d, hl))
        if hl not in direct:
            for d in range(2):
                for which in range(2):
                    x = halves_sum(R.got[2][d, hl, which].astype(F32)) * 0.5
                    R.der3[hl, d, which] = x.astype(BF16)
            start(remote(R.der3.at[hl], R.far3.at[hl], "3d", hl, device(2, False)))

    def step_a(hl):
        far_forward(2, hl, keys2(hl, 0), keys2(hl, 1))

    def forward4():
        for i in range(4):
            for d in range(2):
                arrived(R.got[4].at[i, d], "4", (d, i))
                if i or d:
                    arrived(R.q4.at[i, d], "q4", (d, i))
        q = queries4()
        p, m, total, num = attend(q, keys4(0), keys4(1))
        R.p[4][...] = p
        for i in range(4):
            at = slice(32 * i, 32 * i + 32)
            R.num4[i] = num[at].astype(BF16)
            cut = [x[32 * i + 8 * n : 32 * i + 8 * n + 8] for x in (m, total) for n in range(4)]
            R.stat4[i] = pack_columns(cut)
        R.num4in[turned[0]] = R.num4[0]
        R.stat4in[turned[0]] = R.stat4[0]
        for i in range(1, 4):
            start(remote(R.num4.at[i], R.num4in.at[turned[0]], "n4", i, device(i, False)))
            start(remote(R.stat4.at[i], R.stat4in.at[turned[0]], "t4", i, device(i, False)))

    def take4():
        for i in range(1, 4):
            arrived(R.num4in.at[turned[i]], "n4", i)
            arrived(R.stat4in.at[turned[i]], "t4", i)

    def merge(slot, hl):
        state = None
        scales = {}
        for level in reversed(range(levels)):
            if level == 4:
                stat = R.stat4in[hl]
                m = unpack_columns(stat, 2 * slot, 2)
                total = unpack_columns(stat, 4 + 2 * slot, 2)
                num = R.num4in[hl, pl.ds(16 * slot, 16)].astype(F32)
            else:
                at = plan.span(level)
                m, total, num = (ref[slot, hl, at] for ref in (R.st_m, R.st_l, R.st_num))
            weight = plan.weight(level)
            if state is None:
                scale_a, scale_b = None, jnp.full(m.shape, weight, F32)
                state = (m, total * weight, num * weight)
            else:
                if state[0].shape[0] < m.shape[0]:
                    state = tuple(twice(x) for x in state)
                top = jnp.maximum(state[0], m)
                scale_a = jnp.exp(state[0] - top)
                scale_b = jnp.exp(m - top) * weight
                state = (top, scale_a * state[1] + scale_b * total, scale_a * state[2] + scale_b * num)
            scales[level] = (scale_a, scale_b)
        inverse = 1.0 / state[1]
        att = state[2] * inverse
        give = R.give["o"]
        if slot:
            give[hl] = att.astype(BF16)
        else:
            put_rows("g", core * mine + hl, att)
        g = R.g[slot, hl].astype(F32)
        d = jnp.broadcast_to(jnp.sum(g * att, axis=1, keepdims=True), att.shape)
        c = scales[0][1] * inverse
        at = plan.span(0)
        R.st_g[slot, hl, at] = (g * c).astype(BF16)
        R.st_d[slot, hl, at] = d * c
        scale = scales[0][0] * inverse
        up, up_d = g * scale, d * scale
        for level in range(1, levels):
            scale_a, scale_b = scales[level]
            if up.shape[0] > scale_b.shape[0]:
                up, up_d = halves_sum(up), halves_sum(up_d)
            at = plan.span(level)
            R.st_g[slot, hl, at] = (up * scale_b).astype(BF16)
            R.st_d[slot, hl, at] = up_d * scale_b
            if scale_a is not None:
                up, up_d = up * scale_a, up_d * scale_a

    def put_rows(name, head, x):
        flat = R.flat[name]
        for b in range(16):
            flat[pl.ds(bit_reversed(b, 4) * heads + head, CHUNK, stride=pitch), :] = x[
                b * CHUNK : (b + 1) * CHUNK
            ]

    def far_backward(level, hl, k, v):
        dq, dk, dv = pull(
            R.p[level][hl], both(R.q, hl, level), k, v, both(R.st_g, hl, level), both(R.st_d, hl, level)
        )
        n = plan.kept(level)
        for slot in range(2):
            R.st_dq[slot, hl, plan.span(level)] = dq[slot * n : (slot + 1) * n]
        return dk, dv

    def step_f(hl):
        if hl in direct:
            for d in range(2):
                arrived(R.far3.at[hl, d], "3x", (hl, d))
        else:
            arrived(R.far3.at[hl], "3d", hl)
        far_forward(3, hl, keys3(hl, 0), keys3(hl, 1))

    def step_m(hl):
        for slot in range(2):
            merge(slot, hl)

    def step_b(hl):
        grads = far_backward(3, hl, keys3(hl, 0), keys3(hl, 1))
        for which, x in enumerate(grads):
            for block in range(2):
                for slot in range(2):
                    at = 32 * (2 * block + slot)
                    R.ret[3][hl, block, slot, which] = x[at : at + 32].astype(BF16)
        for block in range(2):
            to = device(3 if block and hl in straight else 2, False)
            start(remote(R.ret[3].at[hl, block], R.back[3].at[hl, block], "b3", (hl, block), to))
        grads = far_backward(2, hl, keys2(hl, 0), keys2(hl, 1))
        for which, x in enumerate(grads):
            for slot in range(2):
                R.dkv2[hl, slot, which] = x[64 * slot : 64 * slot + 64]

    def step_c(hl):
        if hl not in straight:
            arrived(R.back[3].at[hl, 1], "b3", (hl, 1))
        for slot in range(2):
            for which in range(2):
                x = R.dkv2[hl, slot, which]
                if hl not in straight:
                    x = x + twice(R.back[3][hl, 1, slot, which].astype(F32) * 0.5)
                R.ret[2][hl, slot, which] = x.astype(BF16)
        start(remote(R.ret[2].at[hl], R.back[2].at[hl], "b2", hl, device(1, False)))

    def share4():
        for hl in range(mine):
            R.g4out[hl] = both(R.st_g, hl, 4)
            d = both(R.st_d, hl, 4)
            R.d4out[hl] = pack_columns([d[8 * n : 8 * n + 8] for n in range(4)])
        R.g4[0] = R.g4out[turned[0]]
        R.d4[0] = R.d4out[turned[0]]
        for i in range(1, 4):
            start(remote(R.g4out.at[turned[i]], R.g4.at[i], "g4", i, device(i, False)))
            start(remote(R.d4out.at[turned[i]], R.d4.at[i], "d4", i, device(i, False)))

    def backward4():
        for i in range(1, 4):
            arrived(R.g4.at[i], "g4", i)
            arrived(R.d4.at[i], "d4", i)
        q = queries4()
        g = jnp.concatenate([R.g4[i] for i in range(4)], 0)
        d = jnp.concatenate([unpack_columns(R.d4[i], 0, 4) for i in range(4)], 0)
        dq, dk, dv = pull(R.p[4][...], q, keys4(0), keys4(1), g, d)
        for i in range(4):
            R.dq4[i] = dq[32 * i : 32 * i + 32].astype(BF16)
            for which, x in enumerate((dk, dv)):
                for slot in range(2):
                    at = 32 * i + 16 * slot
                    R.ret[4][i, slot, which] = x[at : at + 16].astype(BF16)
        R.dq4in[turned[0]] = R.dq4[0]
        for i in range(1, 4):
            start(remote(R.dq4.at[i], R.dq4in.at[turned[0]], "x4", i, device(i, False)))
        for i in range(4):
            start(remote(R.ret[4].at[i], R.back[4].at[turned[0]], "b4", i, device(4 ^ i, False)))

    def high_forward():
        for level in high:
            for j in range(plan.chips(level)):
                for d in range(2):
                    arrived(R.got[level].at[j, d], "h" + str(level), (j, d))
            for hl in range(mine):
                far_forward(level, hl, keys_high(level, hl, 0), keys_high(level, hl, 1))

    def high_backward():
        for level in high:
            n = plan.chips(level)
            for hl in range(mine):
                grads = far_backward(level, hl, keys_high(level, hl, 0), keys_high(level, hl, 1))
                for which, x in enumerate(grads):
                    for j in range(n):
                        for d in range(2):
                            at = 32 * j + 16 * d
                            R.ret[level][j, d, hl, which] = x[at : at + 16].astype(BF16)
            for j in range(n):
                start(
                    remote(
                        R.ret[level].at[j], R.back[level].at[j], "r" + str(level), j, device(n ^ j, False)
                    )
                )

    def local_backward(hls):
        made = []
        for hl in hls:
            for slot in range(2):
                at = plan.span(0)
                made.append(
                    pull(
                        R.p[0][slot, hl], R.q[slot, hl, near], R.k[slot, hl, near], R.v[slot, hl, near],
                        R.st_g[slot, hl, at], R.st_d[slot, hl, at],
                    )
                )
                at = plan.span(1)
                made.append(
                    pull(
                        R.p[1][1 - slot, hl], R.q[1 - slot, hl, at], R.k[slot, hl, first], R.v[slot, hl, first],
                        R.st_g[1 - slot, hl, at], R.st_d[1 - slot, hl, at],
                    )
                )
        for hl in hls:
            for slot in range(2):
                (dq, dk, dv), (dq1, dk1, dv1) = made.pop(0), made.pop(0)
                R.st_dq[slot, hl, plan.span(0)] = dq
                R.st_dq[1 - slot, hl, plan.span(1)] = dq1
                R.dk[slot, hl] = dk + twice(dk1 * 0.5)
                R.dv[slot, hl] = dv + twice(dv1 * 0.5)

    def hand(index, name, flat, hl, slot, x):
        if slot:
            R.give[name][hl] = x.astype(BF16)
            start(remote(R.give[name].at[hl], R.take[name].at[hl], "fin", (index, hl), sibling))
        else:
            put_rows(flat, core * mine + hl, x)

    def total_q(slot, hl):
        extra = None
        for level in reversed(range(levels)):
            if level == 4:
                x = R.dq4in[hl, pl.ds(16 * slot, 16)].astype(F32)
            else:
                x = R.st_dq[slot, hl, plan.span(level)]
            if level > 4:
                x = run_sums(x, level - 4)
            x = x * 0.5**level
            if extra is None:
                extra = x
            else:
                extra = x + (extra if extra.shape[0] == x.shape[0] else twice(extra))
        return extra * factor

    def total_kv(slot, hl, which):
        extra = R.back[4][hl, slot, which].astype(F32) * 0.5**4
        for level in high:
            x = R.back[level][0, slot, hl, which].astype(F32)
            for j in range(1, plan.chips(level)):
                x = x + R.back[level][j, slot, hl, which].astype(F32)
            extra = extra + run_sums(x, level - 4) * 0.5**level
        x = R.back[3][hl, 0, slot, which].astype(F32)
        if hl in straight:
            x = x + R.back[3][hl, 1, slot, which].astype(F32)
        extra = x * 0.5**3 + twice(extra)
        extra = R.back[2][hl, slot, which].astype(F32) * 0.5**2 + twice(extra)
        x = (R.dk, R.dv)[which][slot, hl] + twice(twice(extra))
        return x if which else x * factor

    def collect(index, name, flat):
        for hl in range(mine):
            arrived(R.take[name].at[hl], "fin", (index, hl))
            put_rows(flat, (1 - core) * mine + hl, R.take[name][hl].astype(F32))

        def body(i, carry):
            x = R.flat[flat][pl.ds(i * pitch, CHUNK * heads), :]
            outs[index][pl.ds(i * CHUNK, CHUNK)] = x.reshape(CHUNK, heads, width).astype(BF16)
            return carry

        lax.fori_loop(0, chunks, body, 0)

    in_pairs(local_forward)
    derive(0)
    step_a(0)
    forward4()
    derive(1)
    step_a(1)
    for d in range(2):
        arrived(R.got[3].at[d], "3", d)
    derive(2)
    step_a(2)
    derive(3)
    step_a(3)
    step_f(0)
    high_forward()
    arrived(R.g.at[1], "ex", 3)
    take4()
    step_m(0)
    step_b(0)
    step_c(0)
    step_f(1)
    step_m(1)
    step_f(2)
    step_m(2)
    step_f(3)
    step_m(3)
    share4()
    for hl in range(mine):
        start(remote(R.give["o"].at[hl], R.take["o"].at[hl], "fin", (0, hl), sibling))
    step_b(1)
    step_c(1)
    step_b(2)
    step_c(2)
    step_b(3)
    step_c(3)
    collect(0, "o", "g")
    high_backward()
    backward4()
    in_pairs(local_backward)
    for i in range(1, 4):
        arrived(R.dq4in.at[turned[i]], "x4", i)
    for hl in range(mine):
        hand(1, "dq", "q", hl, 1, total_q(1, hl))
    for i in range(4):
        arrived(R.back[4].at[turned[i]], "b4", i)
    for level in high:
        for j in range(plan.chips(level)):
            arrived(R.back[level].at[j], "r" + str(level), j)
    for hl in range(mine):
        arrived(R.back[2].at[hl], "b2", hl)
        for block in range(2):
            if block == 0 or hl in straight:
                arrived(R.back[3].at[hl, block], "b3", (hl, block))
        for which, name in enumerate("kv"):
            hand(2 + which, "d" + name, name, hl, 1, total_kv(1, hl, which))
    for hl in range(mine):
        hand(1, "dq", "q", hl, 0, total_q(0, hl))
        for which, name in enumerate("kv"):
            hand(2 + which, "d" + name, name, hl, 0, total_kv(0, hl, which))
    collect(1, "dq", "q")
    collect(2, "dk", "k")
    collect(3, "dv", "v")
    for copy in sent:
        copy.wait_send()


def hand_over(*refs):
    held, made, leave = refs[:4], refs[4:8], refs[8]
    outward = [pltpu.make_async_copy(held[i], made[i], leave.at[i]) for i in range(4)]
    for copy in outward:
        copy.start()
    for copy in outward:
        copy.wait()


def on_device(query_rows, key_rows, value_rows, out_grad):
    rows, heads, width = query_rows.shape
    plan = Plan(rows, heads, width, lax.axis_size("seq"))
    whole = pl.BlockSpec(memory_space=pl.ANY)
    vmem = pl.BlockSpec(memory_space=pltpu.VMEM)
    out = jax.ShapeDtypeStruct(query_rows.shape, BF16)
    made = pl.pallas_call(
        partial(kernel, plan),
        out_shape=(pltpu.VMEM(query_rows.shape, BF16),) * 4,
        in_specs=[whole] * 4,
        out_specs=(vmem,) * 4,
        scratch_shapes=plan.scratch(),
        compiler_params=pltpu.CompilerParams(
            collective_id=0, has_side_effects=True, vmem_limit_bytes=54 << 20
        ),
    )(query_rows, key_rows, value_rows, out_grad)
    return pl.pallas_call(
        hand_over,
        out_shape=(out, out, out, out),
        in_specs=[vmem] * 4,
        out_specs=(whole,) * 4,
        scratch_shapes=[pltpu.SemaphoreType.DMA((4,))],
    )(*[pltpu.with_memory_space_constraint(x, pltpu.VMEM) for x in made])


def solution(mesh):
    spec = P(("groups", "seq"), None, None)
    return jax.shard_map(
        on_device,
        mesh=mesh,
        in_specs=(spec,) * 4,
        out_specs=(spec,) * 4,
        check_vma=False,
    )
```

```python
from functools import partial
from types import SimpleNamespace

import jax
import jax.numpy as jnp
from jax import lax
from jax.experimental import pallas as pl
from jax.experimental.pallas import tpu as pltpu
from jax.sharding import PartitionSpec as P

BLOCK = 128
CHUNK = 16
F32 = jnp.float32
BF16 = jnp.bfloat16
LOG2E = 1.4426950408889634
MESH = pl.DeviceIdType.MESH
OUTS = ("o", "dq", "dk", "dv")


def bit_reversed(value, bits):
    return sum(((value >> bit) & 1) << (bits - 1 - bit) for bit in range(bits))


def dot_nt(a, b):
    return lax.dot_general(a, b, (((1,), (1,)), ((), ())), preferred_element_type=F32)


def dot_nn(a, b):
    return lax.dot_general(a, b, (((1,), (0,)), ((), ())), preferred_element_type=F32)


def dot_tn(a, b):
    return lax.dot_general(a, b, (((0,), (0,)), ((), ())), preferred_element_type=F32)


def flipped(index, mask):
    for bit in range(mask.bit_length()):
        if mask >> bit & 1:
            index = index + (1 << bit) - (2 << bit) * ((index // (1 << bit)) % 2)
    return index


def twice(x):
    return jnp.concatenate([x, x], 0)


def halves_sum(x):
    n = x.shape[0] // 2
    return x[:n] + x[n:]


def run_sums(x, bits):
    n = x.shape[0]
    row = lax.broadcasted_iota(jnp.int32, x.shape, 0)
    for bit in range(bits):
        step = 1 << bit
        up, down = pltpu.roll(x, n - step, 0), pltpu.roll(x, step, 0)
        x = x + jnp.where((row & step) == 0, up, down)
    return x


def pack_columns(parts):
    lane = lax.broadcasted_iota(jnp.int32, (8, 128), 1)
    packed = parts[0]
    for k in range(1, len(parts)):
        packed = jnp.where(lane >= 16 * k, parts[k], packed)
    return packed


def unpack_columns(packed, first, count):
    return jnp.concatenate(
        [jnp.broadcast_to(packed[:, 16 * k : 16 * k + 1], (8, 128)) for k in range(first, first + count)], 0
    )


class Plan:
    def __init__(self, rows, heads, width, devices):
        self.rows, self.heads, self.width, self.devices = rows, heads, width, devices
        self.levels = (rows * devices // BLOCK).bit_length() - 1
        self.mine = heads // 2
        self.pitch = heads * CHUNK + 8
        self.offset = {}
        total = 0
        for level in range(self.levels):
            self.offset[level] = total
            total += self.kept(level)
        self.depth = total
        self.high = list(range(5, self.levels))

    def kept(self, level):
        return max(self.rows >> level, CHUNK)

    def chips(self, level):
        return 1 << (level - 2)

    def weight(self, level):
        return float(1 << min(level, 4))

    def span(self, level):
        return pl.ds(self.offset[level], self.kept(level))

    def scratch(self):
        r, m, w, d = self.rows, self.mine, self.width, self.depth
        flat = (r // CHUNK * self.pitch, w)
        two = r + r // 2
        s = SimpleNamespace()
        vm = pltpu.VMEM
        s.inn = {name: vm((r, self.heads, w), BF16) for name in "kvqg"}
        s.flat = {name: vm(flat, F32) for name in "kvqg"}
        s.k = vm((3, m, two, w), BF16)
        s.v = vm((3, m, two, w), BF16)
        s.q = vm((3, m, d, w), BF16)
        s.g = vm((3, m, r, w), BF16)
        s.st_m, s.st_l, s.st_num, s.st_d, s.st_dq = (vm((2, m, d, w), F32) for _ in range(5))
        s.p, s.snd, s.got, s.ret, s.back = {}, {}, {}, {}, {}
        s.st_g = vm((2, m, d, w), BF16)
        s.p[0] = vm((2, m, r, r), BF16)
        s.p[1] = vm((2, m, BLOCK, BLOCK), BF16)
        s.p[2] = vm((m, BLOCK, BLOCK), BF16)
        s.p[3] = vm((m, BLOCK // 2, BLOCK), BF16)
        s.p[4] = vm((BLOCK, BLOCK), BF16)
        s.dk = vm((2, m, r, w), F32)
        s.dv = vm((2, m, r, w), F32)
        s.snd[2] = vm((2, m, 2, 64, w), BF16)
        s.got[2] = vm((2, m, 2, 64, w), BF16)
        s.snd[3] = vm((2, m, 2, 32, w), BF16)
        s.got[3] = vm((2, m, 2, 32, w), BF16)
        s.der3 = vm((m, 2, 2, 32, w), BF16)
        s.far3 = vm((m, 2, 2, 32, w), BF16)
        s.snd[4] = vm((2, m, 2, 16, w), BF16)
        s.got[4] = vm((m, 2, 2, 16, w), BF16)
        s.q4 = vm((m, 2, 16, w), BF16)
        s.num4 = vm((m, 32, w), BF16)
        s.num4in = vm((m, 32, w), BF16)
        s.stat4 = vm((m, 8, w), F32)
        s.stat4in = vm((m, 8, w), F32)
        s.g4out = vm((m, 32, w), BF16)
        s.g4 = vm((m, 32, w), BF16)
        s.d4out = vm((m, 8, w), F32)
        s.d4 = vm((m, 8, w), F32)
        s.dq4 = vm((m, 32, w), BF16)
        s.dq4in = vm((m, 32, w), BF16)
        s.ret[4] = vm((m, 2, 2, 16, w), BF16)
        s.back[4] = vm((m, 2, 2, 16, w), BF16)
        s.dkv2 = vm((m, 2, 2, 64, w), F32)
        s.ret[2] = vm((m, 2, 2, 64, w), BF16)
        s.back[2] = vm((m, 2, 2, 64, w), BF16)
        s.ret[3] = vm((m, 2, 2, 2, 32, w), BF16)
        s.back[3] = vm((m, 2, 2, 2, 32, w), BF16)
        s.give, s.take = ({name: vm((m, r, w), BF16) for name in OUTS} for _ in range(2))
        for level in self.high:
            n = self.chips(level)
            s.snd[level] = vm((2, m, 2, 16, w), BF16)
            s.got[level] = vm((n, 2, m, 2, 16, w), BF16)
            s.ret[level] = vm((n, 2, m, 2, 16, w), BF16)
            s.back[level] = vm((n, 2, m, 2, 16, w), BF16)
            s.p[level] = vm((m, 32, n * 32), BF16)
        dma = pltpu.SemaphoreType.DMA
        s.sem_in = dma((4,))
        sems = [
            ("ex", (4,)), ("fin", (4, m)), ("2", (2, m)), ("3", (2,)), ("3d", (m,)), ("4", (2, m)),
            ("q4", (2, m)), ("n4", (m,)), ("t4", (m,)), ("g4", (m,)), ("d4", (m,)), ("x4", (m,)), ("b4", (m,)),
            ("b2", (m,)), ("b3", (m, 2)), ("3x", (m, 2)),
        ]
        for level in self.high:
            n = self.chips(level)
            sems += [("h" + str(level), (n, 2)), ("r" + str(level), (n,))]
        s.send, s.recv = ({name: dma(shape) for name, shape in sems} for _ in range(2))
        return vars(s)


def kernel(plan, *refs, **scratch):
    hbm_in, outs = refs[:4], refs[4:8]
    R = SimpleNamespace(**scratch)
    pitch = plan.pitch
    rows, heads, width, mine = plan.rows, plan.heads, plan.width, plan.mine
    levels, high = plan.levels, plan.high
    factor = width ** (-0.5)
    chunks = rows // CHUNK

    me = lax.axis_index("seq")
    core = me % 2
    chip = me // 2
    sibling = me + 1 - 2 * core
    place = chip % 4
    turned = [flipped(place, i) for i in range(4)]

    def device(chip_mask, other):
        return flipped(chip, chip_mask) * 2 + (1 - core if other else core)

    def remote(src, dst, name, index, peer):
        return pltpu.make_async_remote_copy(
            src_ref=src, dst_ref=dst, send_sem=R.send[name].at[index], recv_sem=R.recv[name].at[index],
            device_id={"seq": peer}, device_id_type=MESH,
        )

    def arrived(ref, name, index):
        remote(ref, ref, name, index, sibling).wait_recv()

    fetch = {
        name: pltpu.make_async_copy(ref, R.inn[name], R.sem_in.at[i])
        for i, (name, ref) in enumerate(zip("qkvg", hbm_in))
    }
    for name in "kvqg":
        fetch[name].start()

    peers = [sibling]
    for mask in range(1, 8):
        peers += [device(mask, False), device(mask, True)]
    for level in high:
        for j in range(plan.chips(level)):
            peers += [device(plan.chips(level) ^ j, False), device(plan.chips(level) ^ j, True)]
    barrier = pltpu.get_barrier_semaphore()
    for peer in peers:
        pl.semaphore_signal(barrier, inc=1, device_id={"seq": peer}, device_id_type=MESH)

    direct = (mine - 1,)
    straight = (0, 1, 2, 3)
    sent = []

    def start(copy):
        copy.start()
        sent.append(copy)

    def flush(last):
        while len(sent) > last:
            sent.pop(0).wait_send()

    def spread(names):
        for name in names:
            fetch[name].wait()

        def body(i, carry):
            for name in names:
                x = R.inn[name][pl.ds(i * CHUNK, CHUNK)].astype(F32)
                R.flat[name][pl.ds(i * pitch, CHUNK * heads), :] = x.reshape(CHUNK * heads, width)
            return carry

        lax.fori_loop(0, chunks, body, 0)

    def head_rows(name, head):
        flat = R.flat[name]
        return jnp.concatenate(
            [flat[pl.ds(bit_reversed(b, 4) * heads + head, CHUNK, stride=pitch), :] for b in range(16)], 0
        )

    def coarse(x):
        out = [x]
        for level in range(1, levels):
            if level <= 4:
                out.append(halves_sum(out[-1]))
            else:
                out.append(run_sums(out[4], level - 4))
        return [(y * 0.5**level).astype(BF16) for level, y in enumerate(out)]

    def split_kv(hl, carry):
        for d in range(2):
            head = (core if d == 0 else 1 - core) * mine + hl
            for which, name in enumerate("kv"):
                x = coarse(head_rows(name, head))
                slot = 2 * d
                vars(R)[name][slot, hl, pl.ds(0, rows)] = x[0]
                vars(R)[name][slot, hl, pl.ds(rows, rows // 2)] = x[1]
                for level in range(2, levels):
                    R.snd[level][d, hl, which] = x[level]
        return carry

    def split_qg(hl, carry):
        for d in range(2):
            head = (core if d == 0 else 1 - core) * mine + hl
            slot = 2 * d
            for level, x in enumerate(coarse(head_rows("q", head))):
                R.q[slot, hl, plan.span(level)] = x
            R.g[slot, hl] = head_rows("g", head).astype(BF16)
        return carry

    def attend(q, k, v):
        s = dot_nt(q, k)
        m = jnp.max(s, axis=1, keepdims=True)
        p = jnp.exp2((s - m) * (factor * LOG2E))
        low = p.astype(BF16)
        both_sums = dot_nn(low, jnp.concatenate([v, jnp.ones(v.shape, BF16)], 1))
        m = jnp.broadcast_to(m * factor, (s.shape[0], width))
        return low, m, both_sums[:, width:], both_sums[:, :width]

    def pull(p, q, k, v, g, d):
        dp = dot_nt(g, v)
        lanes = dp.shape[1] // width
        wide = d if lanes == 1 else jnp.concatenate([d] * lanes, 1)
        ds = p * (dp - wide).astype(BF16)
        return dot_nn(ds, k), dot_tn(ds, q), dot_tn(p, g)

    def keep(slot, hl, level, m, total, num):
        at = plan.span(level)
        R.st_m[slot, hl, at] = m
        R.st_l[slot, hl, at] = total
        R.st_num[slot, hl, at] = num

    near = pl.ds(0, rows)
    first = pl.ds(rows, rows // 2)

    def record(slot, hl, level, made):
        p, m, total, num = made
        R.p[level][slot, hl] = p
        keep(slot, hl, level, m, total, num)

    def attend_near(slot, hl):
        return attend(R.q[slot, hl, near], R.k[slot, hl, near], R.v[slot, hl, near])

    def attend_first(slot, hl):
        return attend(R.q[slot, hl, plan.span(1)], R.k[1 - slot, hl, first], R.v[1 - slot, hl, first])

    def in_pairs(body):
        def step(i, carry):
            body([2 * i, 2 * i + 1])
            return carry

        lax.fori_loop(0, mine // 2, step, 0)

    def own_forward(hls):
        made = [attend_near(0, hl) for hl in hls]
        for hl, x in zip(hls, made):
            record(0, hl, 0, x)

    def local_forward(hls):
        made = [(1, hl, 0, attend_near(1, hl)) for hl in hls]
        made += [(slot, hl, 1, attend_first(slot, hl)) for hl in hls for slot in range(2)]
        for x in made:
            record(*x)

    spread("kv")
    lax.fori_loop(0, mine, split_kv, 0)
    spread("qg")
    lax.fori_loop(0, mine, split_qg, 0)
    in_pairs(own_forward)

    pl.semaphore_wait(barrier, len(peers))

    def send2(hl):
        for d in range(2):
            start(remote(R.snd[2].at[d, hl], R.got[2].at[d, hl], "2", (d, hl), device(1, d)))

    for i in reversed(range(4)):
        for d in range(2):
            start(remote(R.snd[4].at[d, turned[i]], R.got[4].at[i, d], "4", (d, i), device(4 ^ i, d)))
            if i or d:
                start(
                    remote(
                        R.q.at[2 * d, turned[i], plan.span(4)], R.q4.at[i, d], "q4", (d, i), device(i, d)
                    )
                )
    R.q4[0, 0] = R.q[0, turned[0], plan.span(4)]
    send2(0)
    start(remote(R.k.at[2], R.k.at[1], "ex", 0, sibling))
    start(remote(R.v.at[2], R.v.at[1], "ex", 1, sibling))
    start(remote(R.q.at[2], R.q.at[1], "ex", 2, sibling))
    start(remote(R.g.at[2], R.g.at[1], "ex", 3, sibling))
    for d in range(2):
        start(remote(R.snd[3].at[d], R.got[3].at[d], "3", d, device(2, d)))
    for hl in range(mine):
        if hl in direct:
            for d in range(2):
                start(remote(R.snd[3].at[d, hl], R.far3.at[hl, d], "3x", (hl, d), device(3, d)))
        if hl:
            send2(hl)
    for level in high:
        for j in range(plan.chips(level)):
            for d in range(2):
                start(
                    remote(
                        R.snd[level].at[d], R.got[level].at[j, d], "h" + str(level), (j, d),
                        device(plan.chips(level) ^ j, d),
                    )
                )

    arrived(R.k.at[1], "ex", 0)
    arrived(R.v.at[1], "ex", 1)
    arrived(R.q.at[1], "ex", 2)
    def both(ref, hl, level):
        return jnp.concatenate([ref[slot, hl, plan.span(level)] for slot in range(2)], 0)

    def keys2(hl, which):
        return jnp.concatenate([R.got[2][d, hl, which] for d in range(2)], 0)

    def keys3(hl, which):
        own = [R.got[3][d, hl, which] for d in range(2)]
        return jnp.concatenate(own + [R.far3[hl, d, which] for d in range(2)], 0)

    def keys4(which):
        return jnp.concatenate([R.got[4][i, d, which] for i in range(4) for d in range(2)], 0)

    def queries4():
        return jnp.concatenate([R.q4[i, d] for i in range(4) for d in range(2)], 0)

    def keys_high(level, hl, which):
        return jnp.concatenate(
            [R.got[level][j, d, hl, which] for j in range(plan.chips(level)) for d in range(2)], 0
        )

    def far_forward(level, hl, k, v):
        p, m, total, num = attend(both(R.q, hl, level), k, v)
        R.p[level][hl] = p
        n = plan.kept(level)
        for slot in range(2):
            at = slice(slot * n, (slot + 1) * n)
            keep(slot, hl, level, m[at], total[at], num[at])

    def derive(hl):
        for d in range(2):
            arrived(R.got[2].at[d, hl], "2", (d, hl))
        if hl not in direct:
            for d in range(2):
                for which in range(2):
                    x = halves_sum(R.got[2][d, hl, which].astype(F32)) * 0.5
                    R.der3[hl, d, which] = x.astype(BF16)
            start(remote(R.der3.at[hl], R.far3.at[hl], "3d", hl, device(2, False)))

    def step_a(hl):
        far_forward(2, hl, keys2(hl, 0), keys2(hl, 1))

    def forward4():
        for i in range(4):
            for d in range(2):
                arrived(R.got[4].at[i, d], "4", (d, i))
                if i or d:
                    arrived(R.q4.at[i, d], "q4", (d, i))
        q = queries4()
        p, m, total, num = attend(q, keys4(0), keys4(1))
        R.p[4][...] = p
        for i in range(4):
            at = slice(32 * i, 32 * i + 32)
            R.num4[i] = num[at].astype(BF16)
            cut = [x[32 * i + 8 * n : 32 * i + 8 * n + 8] for x in (m, total) for n in range(4)]
            R.stat4[i] = pack_columns(cut)
        R.num4in[turned[0]] = R.num4[0]
        R.stat4in[turned[0]] = R.stat4[0]
        for i in range(1, 4):
            start(remote(R.num4.at[i], R.num4in.at[turned[0]], "n4", i, device(i, False)))
            start(remote(R.stat4.at[i], R.stat4in.at[turned[0]], "t4", i, device(i, False)))

    def take4():
        for i in range(1, 4):
            arrived(R.num4in.at[turned[i]], "n4", i)
            arrived(R.stat4in.at[turned[i]], "t4", i)

    def merge(slot, hl):
        state = None
        scales = {}
        for level in reversed(range(levels)):
            if level == 4:
                stat = R.stat4in[hl]
                m = unpack_columns(stat, 2 * slot, 2)
                total = unpack_columns(stat, 4 + 2 * slot, 2)
                num = R.num4in[hl, pl.ds(16 * slot, 16)].astype(F32)
            else:
                at = plan.span(level)
                m, total, num = (ref[slot, hl, at] for ref in (R.st_m, R.st_l, R.st_num))
            weight = plan.weight(level)
            if state is None:
                scale_a, scale_b = None, jnp.full(m.shape, weight, F32)
                state = (m, total * weight, num * weight)
            else:
                if state[0].shape[0] < m.shape[0]:
                    state = tuple(twice(x) for x in state)
                top = jnp.maximum(state[0], m)
                scale_a = jnp.exp(state[0] - top)
                scale_b = jnp.exp(m - top) * weight
                state = (top, scale_a * state[1] + scale_b * total, scale_a * state[2] + scale_b * num)
            scales[level] = (scale_a, scale_b)
        inverse = 1.0 / state[1]
        att = state[2] * inverse
        give = R.give["o"]
        if slot:
            give[hl] = att.astype(BF16)
        else:
            put_rows("g", core * mine + hl, att)
        g = R.g[slot, hl].astype(F32)
        d = jnp.broadcast_to(jnp.sum(g * att, axis=1, keepdims=True), att.shape)
        c = scales[0][1] * inverse
        at = plan.span(0)
        R.st_g[slot, hl, at] = (g * c).astype(BF16)
        R.st_d[slot, hl, at] = d * c
        scale = scales[0][0] * inverse
        up, up_d = g * scale, d * scale
        for level in range(1, levels):
            scale_a, scale_b = scales[level]
            if up.shape[0] > scale_b.shape[0]:
                up, up_d = halves_sum(up), halves_sum(up_d)
            at = plan.span(level)
            R.st_g[slot, hl, at] = (up * scale_b).astype(BF16)
            R.st_d[slot, hl, at] = up_d * scale_b
            if scale_a is not None:
                up, up_d = up * scale_a, up_d * scale_a

    def put_rows(name, head, x):
        flat = R.flat[name]
        for b in range(16):
            flat[pl.ds(bit_reversed(b, 4) * heads + head, CHUNK, stride=pitch), :] = x[
                b * CHUNK : (b + 1) * CHUNK
            ]

    def far_backward(level, hl, k, v):
        dq, dk, dv = pull(
            R.p[level][hl], both(R.q, hl, level), k, v, both(R.st_g, hl, level), both(R.st_d, hl, level)
        )
        n = plan.kept(level)
        for slot in range(2):
            R.st_dq[slot, hl, plan.span(level)] = dq[slot * n : (slot + 1) * n]
        return dk, dv

    def step_f(hl):
        if hl in direct:
            for d in range(2):
                arrived(R.far3.at[hl, d], "3x", (hl, d))
        else:
            arrived(R.far3.at[hl], "3d", hl)
        far_forward(3, hl, keys3(hl, 0), keys3(hl, 1))

    def step_m(hl):
        for slot in range(2):
            merge(slot, hl)

    def step_b(hl):
        grads = far_backward(3, hl, keys3(hl, 0), keys3(hl, 1))
        for which, x in enumerate(grads):
            for block in range(2):
                for slot in range(2):
                    at = 32 * (2 * block + slot)
                    R.ret[3][hl, block, slot, which] = x[at : at + 32].astype(BF16)
        for block in range(2):
            to = device(3 if block and hl in straight else 2, False)
            start(remote(R.ret[3].at[hl, block], R.back[3].at[hl, block], "b3", (hl, block), to))
        grads = far_backward(2, hl, keys2(hl, 0), keys2(hl, 1))
        for which, x in enumerate(grads):
            for slot in range(2):
                R.dkv2[hl, slot, which] = x[64 * slot : 64 * slot + 64]

    def step_c(hl):
        if hl not in straight:
            arrived(R.back[3].at[hl, 1], "b3", (hl, 1))
        for slot in range(2):
            for which in range(2):
                x = R.dkv2[hl, slot, which]
                if hl not in straight:
                    x = x + twice(R.back[3][hl, 1, slot, which].astype(F32) * 0.5)
                R.ret[2][hl, slot, which] = x.astype(BF16)
        start(remote(R.ret[2].at[hl], R.back[2].at[hl], "b2", hl, device(1, False)))

    def share4():
        for hl in range(mine):
            R.g4out[hl] = both(R.st_g, hl, 4)
            d = both(R.st_d, hl, 4)
            R.d4out[hl] = pack_columns([d[8 * n : 8 * n + 8] for n in range(4)])
        R.g4[0] = R.g4out[turned[0]]
        R.d4[0] = R.d4out[turned[0]]
        for i in range(1, 4):
            start(remote(R.g4out.at[turned[i]], R.g4.at[i], "g4", i, device(i, False)))
            start(remote(R.d4out.at[turned[i]], R.d4.at[i], "d4", i, device(i, False)))

    def backward4():
        for i in range(1, 4):
            arrived(R.g4.at[i], "g4", i)
            arrived(R.d4.at[i], "d4", i)
        q = queries4()
        g = jnp.concatenate([R.g4[i] for i in range(4)], 0)
        d = jnp.concatenate([unpack_columns(R.d4[i], 0, 4) for i in range(4)], 0)
        dq, dk, dv = pull(R.p[4][...], q, keys4(0), keys4(1), g, d)
        for i in range(4):
            R.dq4[i] = dq[32 * i : 32 * i + 32].astype(BF16)
            for which, x in enumerate((dk, dv)):
                for slot in range(2):
                    at = 32 * i + 16 * slot
                    R.ret[4][i, slot, which] = x[at : at + 16].astype(BF16)
        R.dq4in[turned[0]] = R.dq4[0]
        for i in range(1, 4):
            start(remote(R.dq4.at[i], R.dq4in.at[turned[0]], "x4", i, device(i, False)))
        for i in range(4):
            start(remote(R.ret[4].at[i], R.back[4].at[turned[0]], "b4", i, device(4 ^ i, False)))

    def high_forward():
        for level in high:
            for j in range(plan.chips(level)):
                for d in range(2):
                    arrived(R.got[level].at[j, d], "h" + str(level), (j, d))
            for hl in range(mine):
                far_forward(level, hl, keys_high(level, hl, 0), keys_high(level, hl, 1))

    def high_backward():
        for level in high:
            n = plan.chips(level)
            for hl in range(mine):
                grads = far_backward(level, hl, keys_high(level, hl, 0), keys_high(level, hl, 1))
                for which, x in enumerate(grads):
                    for j in range(n):
                        for d in range(2):
                            at = 32 * j + 16 * d
                            R.ret[level][j, d, hl, which] = x[at : at + 16].astype(BF16)
            for j in range(n):
                start(
                    remote(
                        R.ret[level].at[j], R.back[level].at[j], "r" + str(level), j, device(n ^ j, False)
                    )
                )

    def local_backward(hls):
        made = []
        for hl in hls:
            for slot in range(2):
                at = plan.span(0)
                made.append(
                    pull(
                        R.p[0][slot, hl], R.q[slot, hl, near], R.k[slot, hl, near], R.v[slot, hl, near],
                        R.st_g[slot, hl, at], R.st_d[slot, hl, at],
                    )
                )
                at = plan.span(1)
                made.append(
                    pull(
                        R.p[1][1 - slot, hl], R.q[1 - slot, hl, at], R.k[slot, hl, first], R.v[slot, hl, first],
                        R.st_g[1 - slot, hl, at], R.st_d[1 - slot, hl, at],
                    )
                )
        for hl in hls:
            for slot in range(2):
                (dq, dk, dv), (dq1, dk1, dv1) = made.pop(0), made.pop(0)
                R.st_dq[slot, hl, plan.span(0)] = dq
                R.st_dq[1 - slot, hl, plan.span(1)] = dq1
                R.dk[slot, hl] = dk + twice(dk1 * 0.5)
                R.dv[slot, hl] = dv + twice(dv1 * 0.5)

    def hand(index, name, flat, hl, slot, x):
        if slot:
            R.give[name][hl] = x.astype(BF16)
            start(remote(R.give[name].at[hl], R.take[name].at[hl], "fin", (index, hl), sibling))
        else:
            put_rows(flat, core * mine + hl, x)

    def total_q(slot, hl):
        extra = None
        for level in reversed(range(levels)):
            if level == 4:
                x = R.dq4in[hl, pl.ds(16 * slot, 16)].astype(F32)
            else:
                x = R.st_dq[slot, hl, plan.span(level)]
            if level > 4:
                x = run_sums(x, level - 4)
            x = x * 0.5**level
            if extra is None:
                extra = x
            else:
                extra = x + (extra if extra.shape[0] == x.shape[0] else twice(extra))
        return extra * factor

    def total_kv(slot, hl, which):
        extra = R.back[4][hl, slot, which].astype(F32) * 0.5**4
        for level in high:
            x = R.back[level][0, slot, hl, which].astype(F32)
            for j in range(1, plan.chips(level)):
                x = x + R.back[level][j, slot, hl, which].astype(F32)
            extra = extra + run_sums(x, level - 4) * 0.5**level
        x = R.back[3][hl, 0, slot, which].astype(F32)
        if hl in straight:
            x = x + R.back[3][hl, 1, slot, which].astype(F32)
        extra = x * 0.5**3 + twice(extra)
        extra = R.back[2][hl, slot, which].astype(F32) * 0.5**2 + twice(extra)
        x = (R.dk, R.dv)[which][slot, hl] + twice(twice(extra))
        return x if which else x * factor

    def collect(index, name, flat):
        for hl in range(mine):
            arrived(R.take[name].at[hl], "fin", (index, hl))
            put_rows(flat, (1 - core) * mine + hl, R.take[name][hl].astype(F32))

        def body(i, carry):
            x = R.flat[flat][pl.ds(i * pitch, CHUNK * heads), :]
            outs[index][pl.ds(i * CHUNK, CHUNK)] = x.reshape(CHUNK, heads, width).astype(BF16)
            return carry

        lax.fori_loop(0, chunks, body, 0)

    in_pairs(local_forward)
    derive(0)
    step_a(0)
    forward4()
    derive(1)
    step_a(1)
    for d in range(2):
        arrived(R.got[3].at[d], "3", d)
    derive(2)
    step_a(2)
    derive(3)
    step_a(3)
    step_f(0)
    high_forward()
    arrived(R.g.at[1], "ex", 3)
    take4()
    step_m(0)
    step_b(0)
    step_c(0)
    step_f(1)
    step_m(1)
    step_f(2)
    step_m(2)
    step_f(3)
    step_m(3)
    share4()
    for hl in range(mine):
        start(remote(R.give["o"].at[hl], R.take["o"].at[hl], "fin", (0, hl), sibling))
    step_b(1)
    step_c(1)
    step_b(2)
    step_c(2)
    step_b(3)
    step_c(3)
    collect(0, "o", "g")
    high_backward()
    backward4()
    in_pairs(local_backward)
    flush(7)
    for i in range(1, 4):
        arrived(R.dq4in.at[turned[i]], "x4", i)
    for hl in range(mine):
        hand(1, "dq", "q", hl, 1, total_q(1, hl))
    for i in range(4):
        arrived(R.back[4].at[turned[i]], "b4", i)
    for level in high:
        for j in range(plan.chips(level)):
            arrived(R.back[level].at[j], "r" + str(level), j)
    for hl in range(mine):
        arrived(R.back[2].at[hl], "b2", hl)
        for block in range(2):
            if block == 0 or hl in straight:
                arrived(R.back[3].at[hl, block], "b3", (hl, block))
        for which, name in enumerate("kv"):
            hand(2 + which, "d" + name, name, hl, 1, total_kv(1, hl, which))
    for hl in range(mine):
        hand(1, "dq", "q", hl, 0, total_q(0, hl))
        for which, name in enumerate("kv"):
            hand(2 + which, "d" + name, name, hl, 0, total_kv(0, hl, which))
    collect(1, "dq", "q")
    collect(2, "dk", "k")
    collect(3, "dv", "v")
    for copy in sent:
        copy.wait_send()


def hand_over(*refs):
    held, made, leave = refs[:4], refs[4:8], refs[8]
    outward = [pltpu.make_async_copy(held[i], made[i], leave.at[i]) for i in range(4)]
    for copy in outward:
        copy.start()
    for copy in outward:
        copy.wait()


def on_device(query_rows, key_rows, value_rows, out_grad):
    rows, heads, width = query_rows.shape
    plan = Plan(rows, heads, width, lax.axis_size("seq"))
    whole = pl.BlockSpec(memory_space=pl.ANY)
    vmem = pl.BlockSpec(memory_space=pltpu.VMEM)
    out = jax.ShapeDtypeStruct(query_rows.shape, BF16)
    made = pl.pallas_call(
        partial(kernel, plan),
        out_shape=(pltpu.VMEM(query_rows.shape, BF16),) * 4,
        in_specs=[whole] * 4,
        out_specs=(vmem,) * 4,
        scratch_shapes=plan.scratch(),
        compiler_params=pltpu.CompilerParams(
            collective_id=0, has_side_effects=True, vmem_limit_bytes=54 << 20
        ),
    )(query_rows, key_rows, value_rows, out_grad)
    return pl.pallas_call(
        hand_over,
        out_shape=(out, out, out, out),
        in_specs=[vmem] * 4,
        out_specs=(whole,) * 4,
        scratch_shapes=[pltpu.SemaphoreType.DMA((4,))],
    )(*[pltpu.with_memory_space_constraint(x, pltpu.VMEM) for x in made])


def solution(mesh):
    spec = P(("groups", "seq"), None, None)
    return jax.shard_map(
        on_device,
        mesh=mesh,
        in_specs=(spec,) * 4,
        out_specs=(spec,) * 4,
        check_vma=False,
    )
```

```python
from functools import partial
from types import SimpleNamespace

import jax
import jax.numpy as jnp
from jax import lax
from jax.experimental import pallas as pl
from jax.experimental.pallas import tpu as pltpu
from jax.sharding import PartitionSpec as P

BLOCK = 128
CHUNK = 16
F32 = jnp.float32
BF16 = jnp.bfloat16
LOG2E = 1.4426950408889634
MESH = pl.DeviceIdType.MESH
OUTS = ("o", "dq", "dk", "dv")


def bit_reversed(value, bits):
    return sum(((value >> bit) & 1) << (bits - 1 - bit) for bit in range(bits))


def dot_nt(a, b):
    return lax.dot_general(a, b, (((1,), (1,)), ((), ())), preferred_element_type=F32)


def dot_nn(a, b):
    return lax.dot_general(a, b, (((1,), (0,)), ((), ())), preferred_element_type=F32)


def dot_tn(a, b):
    return lax.dot_general(a, b, (((0,), (0,)), ((), ())), preferred_element_type=F32)


def flipped(index, mask):
    for bit in range(mask.bit_length()):
        if mask >> bit & 1:
            index = index + (1 << bit) - (2 << bit) * ((index // (1 << bit)) % 2)
    return index


def twice(x):
    return jnp.concatenate([x, x], 0)


def halves_sum(x):
    n = x.shape[0] // 2
    return x[:n] + x[n:]


def run_sums(x, bits):
    n = x.shape[0]
    row = lax.broadcasted_iota(jnp.int32, x.shape, 0)
    for bit in range(bits):
        step = 1 << bit
        up, down = pltpu.roll(x, n - step, 0), pltpu.roll(x, step, 0)
        x = x + jnp.where((row & step) == 0, up, down)
    return x


def pack_columns(parts):
    lane = lax.broadcasted_iota(jnp.int32, (8, 128), 1)
    packed = parts[0]
    for k in range(1, len(parts)):
        packed = jnp.where(lane >= 16 * k, parts[k], packed)
    return packed


def unpack_columns(packed, first, count):
    return jnp.concatenate(
        [jnp.broadcast_to(packed[:, 16 * k : 16 * k + 1], (8, 128)) for k in range(first, first + count)], 0
    )


class Plan:
    def __init__(self, rows, heads, width, devices):
        self.rows, self.heads, self.width, self.devices = rows, heads, width, devices
        self.levels = (rows * devices // BLOCK).bit_length() - 1
        self.mine = heads // 2
        self.pitch = heads * CHUNK + 8
        self.offset = {}
        total = 0
        for level in range(self.levels):
            self.offset[level] = total
            total += self.kept(level)
        self.depth = total
        self.high = list(range(5, self.levels))

    def kept(self, level):
        return max(self.rows >> level, CHUNK)

    def chips(self, level):
        return 1 << (level - 2)

    def weight(self, level):
        return float(1 << min(level, 4))

    def span(self, level):
        return pl.ds(self.offset[level], self.kept(level))

    def scratch(self):
        r, m, w, d = self.rows, self.mine, self.width, self.depth
        flat = (r // CHUNK * self.pitch, w)
        two = r + r // 2
        s = SimpleNamespace()
        vm = pltpu.VMEM
        s.inn = {name: vm((r, self.heads, w), BF16) for name in "kvqg"}
        s.flat = {name: vm(flat, F32) for name in "kvqg"}
        s.k = vm((3, m, two, w), BF16)
        s.v = vm((3, m, two, w), BF16)
        s.q = vm((3, m, d, w), BF16)
        s.g = vm((3, m, r, w), BF16)
        s.st_m, s.st_l, s.st_num, s.st_d, s.st_dq = (vm((2, m, d, w), F32) for _ in range(5))
        s.p, s.snd, s.got, s.ret, s.back = {}, {}, {}, {}, {}
        s.st_g = vm((2, m, d, w), BF16)
        s.p[0] = vm((2, m, r, r), BF16)
        s.p[1] = vm((2, m, BLOCK, BLOCK), BF16)
        s.p[2] = vm((m, BLOCK, BLOCK), BF16)
        s.p[3] = vm((m, BLOCK // 2, BLOCK), BF16)
        s.p[4] = vm((BLOCK, BLOCK), BF16)
        s.dk = vm((2, m, r, w), F32)
        s.dv = vm((2, m, r, w), F32)
        s.snd[2] = vm((2, m, 2, 64, w), BF16)
        s.got[2] = vm((2, m, 2, 64, w), BF16)
        s.snd[3] = vm((2, m, 2, 32, w), BF16)
        s.got[3] = vm((2, m, 2, 32, w), BF16)
        s.der3 = vm((m, 2, 2, 32, w), BF16)
        s.far3 = vm((m, 2, 2, 32, w), BF16)
        s.snd[4] = vm((2, m, 2, 16, w), BF16)
        s.got[4] = vm((m, 2, 2, 16, w), BF16)
        s.q4 = vm((m, 2, 16, w), BF16)
        s.num4 = vm((m, 32, w), BF16)
        s.num4in = vm((m, 32, w), BF16)
        s.stat4 = vm((m, 8, w), F32)
        s.stat4in = vm((m, 8, w), F32)
        s.g4out = vm((m, 32, w), BF16)
        s.g4 = vm((m, 32, w), BF16)
        s.d4out = vm((m, 8, w), F32)
        s.d4 = vm((m, 8, w), F32)
        s.dq4 = vm((m, 32, w), BF16)
        s.dq4in = vm((m, 32, w), BF16)
        s.ret[4] = vm((m, 2, 2, 16, w), BF16)
        s.back[4] = vm((m, 2, 2, 16, w), BF16)
        s.dkv2 = vm((m, 2, 2, 64, w), F32)
        s.ret[2] = vm((m, 2, 2, 64, w), BF16)
        s.back[2] = vm((m, 2, 2, 64, w), BF16)
        s.ret[3] = vm((m, 2, 2, 2, 32, w), BF16)
        s.back[3] = vm((m, 2, 2, 2, 32, w), BF16)
        s.give, s.take = ({name: vm((m, r, w), BF16) for name in OUTS} for _ in range(2))
        for level in self.high:
            n = self.chips(level)
            s.snd[level] = vm((2, m, 2, 16, w), BF16)
            s.got[level] = vm((n, 2, m, 2, 16, w), BF16)
            s.ret[level] = vm((n, 2, m, 2, 16, w), BF16)
            s.back[level] = vm((n, 2, m, 2, 16, w), BF16)
            s.p[level] = vm((m, 32, n * 32), BF16)
        dma = pltpu.SemaphoreType.DMA
        s.sem_in = dma((4,))
        sems = [
            ("ex", (4,)), ("fin", (4, m)), ("2", (2, m)), ("3", (2,)), ("3d", (m,)), ("4", (2, m)),
            ("q4", (2, m)), ("n4", (m,)), ("t4", (m,)), ("g4", (m,)), ("d4", (m,)), ("x4", (m,)), ("b4", (m,)),
            ("b2", (m,)), ("b3", (m, 2)), ("3x", (m, 2)),
        ]
        for level in self.high:
            n = self.chips(level)
            sems += [("h" + str(level), (n, 2)), ("r" + str(level), (n,))]
        s.send, s.recv = ({name: dma(shape) for name, shape in sems} for _ in range(2))
        return vars(s)


def kernel(plan, *refs, **scratch):
    hbm_in, outs = refs[:4], refs[4:8]
    R = SimpleNamespace(**scratch)
    pitch = plan.pitch
    rows, heads, width, mine = plan.rows, plan.heads, plan.width, plan.mine
    levels, high = plan.levels, plan.high
    factor = width ** (-0.5)
    chunks = rows // CHUNK

    me = lax.axis_index("seq")
    core = me % 2
    chip = me // 2
    sibling = me + 1 - 2 * core
    place = chip % 4
    turned = [flipped(place, i) for i in range(4)]

    def device(chip_mask, other):
        return flipped(chip, chip_mask) * 2 + (1 - core if other else core)

    def remote(src, dst, name, index, peer):
        return pltpu.make_async_remote_copy(
            src_ref=src, dst_ref=dst, send_sem=R.send[name].at[index], recv_sem=R.recv[name].at[index],
            device_id={"seq": peer}, device_id_type=MESH,
        )

    def arrived(ref, name, index):
        remote(ref, ref, name, index, sibling).wait_recv()

    fetch = {
        name: pltpu.make_async_copy(ref, R.inn[name], R.sem_in.at[i])
        for i, (name, ref) in enumerate(zip("qkvg", hbm_in))
    }
    for name in "kvqg":
        fetch[name].start()

    peers = [sibling]
    for mask in range(1, 8):
        peers += [device(mask, False), device(mask, True)]
    for level in high:
        for j in range(plan.chips(level)):
            peers += [device(plan.chips(level) ^ j, False), device(plan.chips(level) ^ j, True)]
    barrier = pltpu.get_barrier_semaphore()
    for peer in peers:
        pl.semaphore_signal(barrier, inc=1, device_id={"seq": peer}, device_id_type=MESH)

    direct = (mine - 1,)
    straight = (0, 1, 2, 3)
    sent = []

    def start(copy):
        copy.start()
        sent.append(copy)

    def flush(last):
        while len(sent) > last:
            sent.pop(0).wait_send()

    def spread(names):
        for name in names:
            fetch[name].wait()

        def body(i, carry):
            for name in names:
                x = R.inn[name][pl.ds(i * CHUNK, CHUNK)].astype(F32)
                R.flat[name][pl.ds(i * pitch, CHUNK * heads), :] = x.reshape(CHUNK * heads, width)
            return carry

        lax.fori_loop(0, chunks, body, 0)

    def head_rows(name, head):
        flat = R.flat[name]
        return jnp.concatenate(
            [flat[pl.ds(bit_reversed(b, 4) * heads + head, CHUNK, stride=pitch), :] for b in range(16)], 0
        )

    def coarse(x):
        out = [x]
        for level in range(1, levels):
            if level <= 4:
                out.append(halves_sum(out[-1]))
            else:
                out.append(run_sums(out[4], level - 4))
        return [(y * 0.5**level).astype(BF16) for level, y in enumerate(out)]

    def split_kv(hl, carry):
        for d in range(2):
            head = (core if d == 0 else 1 - core) * mine + hl
            for which, name in enumerate("kv"):
                x = coarse(head_rows(name, head))
                slot = 2 * d
                vars(R)[name][slot, hl, pl.ds(0, rows)] = x[0]
                vars(R)[name][slot, hl, pl.ds(rows, rows // 2)] = x[1]
                for level in range(2, levels):
                    R.snd[level][d, hl, which] = x[level]
        return carry

    def split_qg(hl, carry):
        for d in range(2):
            head = (core if d == 0 else 1 - core) * mine + hl
            slot = 2 * d
            for level, x in enumerate(coarse(head_rows("q", head))):
                R.q[slot, hl, plan.span(level)] = x
            R.g[slot, hl] = head_rows("g", head).astype(BF16)
        return carry

    def attend(q, k, v):
        s = dot_nt(q, k)
        m = jnp.max(s, axis=1, keepdims=True)
        p = jnp.exp2((s - m) * (factor * LOG2E))
        low = p.astype(BF16)
        both_sums = dot_nn(low, jnp.concatenate([v, jnp.ones(v.shape, BF16)], 1))
        m = jnp.broadcast_to(m * factor, (s.shape[0], width))
        return low, m, both_sums[:, width:], both_sums[:, :width]

    def pull(p, q, k, v, g, d):
        dp = dot_nt(g, v)
        lanes = dp.shape[1] // width
        wide = d if lanes == 1 else jnp.concatenate([d] * lanes, 1)
        ds = p * (dp - wide).astype(BF16)
        return dot_nn(ds, k), dot_tn(ds, q), dot_tn(p, g)

    def keep(slot, hl, level, m, total, num):
        at = plan.span(level)
        R.st_m[slot, hl, at] = m
        R.st_l[slot, hl, at] = total
        R.st_num[slot, hl, at] = num

    near = pl.ds(0, rows)
    first = pl.ds(rows, rows // 2)

    def record(slot, hl, level, made):
        p, m, total, num = made
        R.p[level][slot, hl] = p
        keep(slot, hl, level, m, total, num)

    def attend_near(slot, hl):
        return attend(R.q[slot, hl, near], R.k[slot, hl, near], R.v[slot, hl, near])

    def attend_first(slot, hl):
        return attend(R.q[slot, hl, plan.span(1)], R.k[1 - slot, hl, first], R.v[1 - slot, hl, first])

    def in_pairs(body):
        def step(i, carry):
            body([2 * i, 2 * i + 1])
            return carry

        lax.fori_loop(0, mine // 2, step, 0)

    def own_forward(hls):
        made = [attend_near(0, hl) for hl in hls]
        for hl, x in zip(hls, made):
            record(0, hl, 0, x)

    def local_forward(hls):
        made = [(1, hl, 0, attend_near(1, hl)) for hl in hls]
        made += [(slot, hl, 1, attend_first(slot, hl)) for hl in hls for slot in range(2)]
        for x in made:
            record(*x)

    spread("kv")
    lax.fori_loop(0, mine, split_kv, 0)
    spread("qg")
    lax.fori_loop(0, mine, split_qg, 0)
    own_forward(list(range(mine)))

    pl.semaphore_wait(barrier, len(peers))

    def send2(hl):
        for d in range(2):
            start(remote(R.snd[2].at[d, hl], R.got[2].at[d, hl], "2", (d, hl), device(1, d)))

    for i in reversed(range(4)):
        for d in range(2):
            start(remote(R.snd[4].at[d, turned[i]], R.got[4].at[i, d], "4", (d, i), device(4 ^ i, d)))
            if i or d:
                start(
                    remote(
                        R.q.at[2 * d, turned[i], plan.span(4)], R.q4.at[i, d], "q4", (d, i), device(i, d)
                    )
                )
    R.q4[0, 0] = R.q[0, turned[0], plan.span(4)]
    send2(0)
    start(remote(R.k.at[2], R.k.at[1], "ex", 0, sibling))
    start(remote(R.v.at[2], R.v.at[1], "ex", 1, sibling))
    start(remote(R.q.at[2], R.q.at[1], "ex", 2, sibling))
    start(remote(R.g.at[2], R.g.at[1], "ex", 3, sibling))
    for d in range(2):
        start(remote(R.snd[3].at[d], R.got[3].at[d], "3", d, device(2, d)))
    for hl in range(mine):
        if hl in direct:
            for d in range(2):
                start(remote(R.snd[3].at[d, hl], R.far3.at[hl, d], "3x", (hl, d), device(3, d)))
        if hl:
            send2(hl)
    for level in high:
        for j in range(plan.chips(level)):
            for d in range(2):
                start(
                    remote(
                        R.snd[level].at[d], R.got[level].at[j, d], "h" + str(level), (j, d),
                        device(plan.chips(level) ^ j, d),
                    )
                )

    arrived(R.k.at[1], "ex", 0)
    arrived(R.v.at[1], "ex", 1)
    arrived(R.q.at[1], "ex", 2)
    def both(ref, hl, level):
        return jnp.concatenate([ref[slot, hl, plan.span(level)] for slot in range(2)], 0)

    def keys2(hl, which):
        return jnp.concatenate([R.got[2][d, hl, which] for d in range(2)], 0)

    def keys3(hl, which):
        own = [R.got[3][d, hl, which] for d in range(2)]
        return jnp.concatenate(own + [R.far3[hl, d, which] for d in range(2)], 0)

    def keys4(which):
        return jnp.concatenate([R.got[4][i, d, which] for i in range(4) for d in range(2)], 0)

    def queries4():
        return jnp.concatenate([R.q4[i, d] for i in range(4) for d in range(2)], 0)

    def keys_high(level, hl, which):
        return jnp.concatenate(
            [R.got[level][j, d, hl, which] for j in range(plan.chips(level)) for d in range(2)], 0
        )

    def far_forward(level, hl, k, v):
        p, m, total, num = attend(both(R.q, hl, level), k, v)
        R.p[level][hl] = p
        n = plan.kept(level)
        for slot in range(2):
            at = slice(slot * n, (slot + 1) * n)
            keep(slot, hl, level, m[at], total[at], num[at])

    def derive(hl):
        for d in range(2):
            arrived(R.got[2].at[d, hl], "2", (d, hl))
        if hl not in direct:
            for d in range(2):
                for which in range(2):
                    x = halves_sum(R.got[2][d, hl, which].astype(F32)) * 0.5
                    R.der3[hl, d, which] = x.astype(BF16)
            start(remote(R.der3.at[hl], R.far3.at[hl], "3d", hl, device(2, False)))

    def step_a(hl):
        far_forward(2, hl, keys2(hl, 0), keys2(hl, 1))

    def forward4():
        for i in range(4):
            for d in range(2):
                arrived(R.got[4].at[i, d], "4", (d, i))
                if i or d:
                    arrived(R.q4.at[i, d], "q4", (d, i))
        q = queries4()
        p, m, total, num = attend(q, keys4(0), keys4(1))
        R.p[4][...] = p
        for i in range(4):
            at = slice(32 * i, 32 * i + 32)
            R.num4[i] = num[at].astype(BF16)
            cut = [x[32 * i + 8 * n : 32 * i + 8 * n + 8] for x in (m, total) for n in range(4)]
            R.stat4[i] = pack_columns(cut)
        R.num4in[turned[0]] = R.num4[0]
        R.stat4in[turned[0]] = R.stat4[0]
        for i in range(1, 4):
            start(remote(R.num4.at[i], R.num4in.at[turned[0]], "n4", i, device(i, False)))
            start(remote(R.stat4.at[i], R.stat4in.at[turned[0]], "t4", i, device(i, False)))

    def take4():
        for i in range(1, 4):
            arrived(R.num4in.at[turned[i]], "n4", i)
            arrived(R.stat4in.at[turned[i]], "t4", i)

    def merge(slot, hl):
        state = None
        scales = {}
        for level in reversed(range(levels)):
            if level == 4:
                stat = R.stat4in[hl]
                m = unpack_columns(stat, 2 * slot, 2)
                total = unpack_columns(stat, 4 + 2 * slot, 2)
                num = R.num4in[hl, pl.ds(16 * slot, 16)].astype(F32)
            else:
                at = plan.span(level)
                m, total, num = (ref[slot, hl, at] for ref in (R.st_m, R.st_l, R.st_num))
            weight = plan.weight(level)
            if state is None:
                scale_a, scale_b = None, jnp.full(m.shape, weight, F32)
                state = (m, total * weight, num * weight)
            else:
                if state[0].shape[0] < m.shape[0]:
                    state = tuple(twice(x) for x in state)
                top = jnp.maximum(state[0], m)
                scale_a = jnp.exp(state[0] - top)
                scale_b = jnp.exp(m - top) * weight
                state = (top, scale_a * state[1] + scale_b * total, scale_a * state[2] + scale_b * num)
            scales[level] = (scale_a, scale_b)
        inverse = 1.0 / state[1]
        att = state[2] * inverse
        give = R.give["o"]
        if slot:
            give[hl] = att.astype(BF16)
        else:
            put_rows("g", core * mine + hl, att)
        g = R.g[slot, hl].astype(F32)
        d = jnp.broadcast_to(jnp.sum(g * att, axis=1, keepdims=True), att.shape)
        c = scales[0][1] * inverse
        at = plan.span(0)
        R.st_g[slot, hl, at] = (g * c).astype(BF16)
        R.st_d[slot, hl, at] = d * c
        scale = scales[0][0] * inverse
        up, up_d = g * scale, d * scale
        for level in range(1, levels):
            scale_a, scale_b = scales[level]
            if up.shape[0] > scale_b.shape[0]:
                up, up_d = halves_sum(up), halves_sum(up_d)
            at = plan.span(level)
            R.st_g[slot, hl, at] = (up * scale_b).astype(BF16)
            R.st_d[slot, hl, at] = up_d * scale_b
            if scale_a is not None:
                up, up_d = up * scale_a, up_d * scale_a

    def put_rows(name, head, x):
        flat = R.flat[name]
        for b in range(16):
            flat[pl.ds(bit_reversed(b, 4) * heads + head, CHUNK, stride=pitch), :] = x[
                b * CHUNK : (b + 1) * CHUNK
            ]

    def far_backward(level, hl, k, v):
        dq, dk, dv = pull(
            R.p[level][hl], both(R.q, hl, level), k, v, both(R.st_g, hl, level), both(R.st_d, hl, level)
        )
        n = plan.kept(level)
        for slot in range(2):
            R.st_dq[slot, hl, plan.span(level)] = dq[slot * n : (slot + 1) * n]
        return dk, dv

    def step_f(hl):
        if hl in direct:
            for d in range(2):
                arrived(R.far3.at[hl, d], "3x", (hl, d))
        else:
            arrived(R.far3.at[hl], "3d", hl)
        far_forward(3, hl, keys3(hl, 0), keys3(hl, 1))

    def step_m(hl):
        for slot in range(2):
            merge(slot, hl)

    def step_b(hl):
        grads = far_backward(3, hl, keys3(hl, 0), keys3(hl, 1))
        for which, x in enumerate(grads):
            for block in range(2):
                for slot in range(2):
                    at = 32 * (2 * block + slot)
                    R.ret[3][hl, block, slot, which] = x[at : at + 32].astype(BF16)
        for block in range(2):
            to = device(3 if block and hl in straight else 2, False)
            start(remote(R.ret[3].at[hl, block], R.back[3].at[hl, block], "b3", (hl, block), to))
        grads = far_backward(2, hl, keys2(hl, 0), keys2(hl, 1))
        for which, x in enumerate(grads):
            for slot in range(2):
                R.dkv2[hl, slot, which] = x[64 * slot : 64 * slot + 64]

    def step_c(hl):
        if hl not in straight:
            arrived(R.back[3].at[hl, 1], "b3", (hl, 1))
        for slot in range(2):
            for which in range(2):
                x = R.dkv2[hl, slot, which]
                if hl not in straight:
                    x = x + twice(R.back[3][hl, 1, slot, which].astype(F32) * 0.5)
                R.ret[2][hl, slot, which] = x.astype(BF16)
        start(remote(R.ret[2].at[hl], R.back[2].at[hl], "b2", hl, device(1, False)))

    def share4():
        for hl in range(mine):
            R.g4out[hl] = both(R.st_g, hl, 4)
            d = both(R.st_d, hl, 4)
            R.d4out[hl] = pack_columns([d[8 * n : 8 * n + 8] for n in range(4)])
        R.g4[0] = R.g4out[turned[0]]
        R.d4[0] = R.d4out[turned[0]]
        for i in range(1, 4):
            start(remote(R.g4out.at[turned[i]], R.g4.at[i], "g4", i, device(i, False)))
            start(remote(R.d4out.at[turned[i]], R.d4.at[i], "d4", i, device(i, False)))

    def backward4():
        for i in range(1, 4):
            arrived(R.g4.at[i], "g4", i)
            arrived(R.d4.at[i], "d4", i)
        q = queries4()
        g = jnp.concatenate([R.g4[i] for i in range(4)], 0)
        d = jnp.concatenate([unpack_columns(R.d4[i], 0, 4) for i in range(4)], 0)
        dq, dk, dv = pull(R.p[4][...], q, keys4(0), keys4(1), g, d)
        for i in range(4):
            R.dq4[i] = dq[32 * i : 32 * i + 32].astype(BF16)
            for which, x in enumerate((dk, dv)):
                for slot in range(2):
                    at = 32 * i + 16 * slot
                    R.ret[4][i, slot, which] = x[at : at + 16].astype(BF16)
        R.dq4in[turned[0]] = R.dq4[0]
        for i in range(1, 4):
            start(remote(R.dq4.at[i], R.dq4in.at[turned[0]], "x4", i, device(i, False)))
        for i in range(4):
            start(remote(R.ret[4].at[i], R.back[4].at[turned[0]], "b4", i, device(4 ^ i, False)))

    def high_forward():
        for level in high:
            for j in range(plan.chips(level)):
                for d in range(2):
                    arrived(R.got[level].at[j, d], "h" + str(level), (j, d))
            for hl in range(mine):
                far_forward(level, hl, keys_high(level, hl, 0), keys_high(level, hl, 1))

    def high_backward():
        for level in high:
            n = plan.chips(level)
            for hl in range(mine):
                grads = far_backward(level, hl, keys_high(level, hl, 0), keys_high(level, hl, 1))
                for which, x in enumerate(grads):
                    for j in range(n):
                        for d in range(2):
                            at = 32 * j + 16 * d
                            R.ret[level][j, d, hl, which] = x[at : at + 16].astype(BF16)
            for j in range(n):
                start(
                    remote(
                        R.ret[level].at[j], R.back[level].at[j], "r" + str(level), j, device(n ^ j, False)
                    )
                )

    def local_backward(hls):
        made = []
        for hl in hls:
            for slot in range(2):
                at = plan.span(0)
                made.append(
                    pull(
                        R.p[0][slot, hl], R.q[slot, hl, near], R.k[slot, hl, near], R.v[slot, hl, near],
                        R.st_g[slot, hl, at], R.st_d[slot, hl, at],
                    )
                )
                at = plan.span(1)
                made.append(
                    pull(
                        R.p[1][1 - slot, hl], R.q[1 - slot, hl, at], R.k[slot, hl, first], R.v[slot, hl, first],
                        R.st_g[1 - slot, hl, at], R.st_d[1 - slot, hl, at],
                    )
                )
        for hl in hls:
            for slot in range(2):
                (dq, dk, dv), (dq1, dk1, dv1) = made.pop(0), made.pop(0)
                R.st_dq[slot, hl, plan.span(0)] = dq
                R.st_dq[1 - slot, hl, plan.span(1)] = dq1
                R.dk[slot, hl] = dk + twice(dk1 * 0.5)
                R.dv[slot, hl] = dv + twice(dv1 * 0.5)

    def hand(index, name, flat, hl, slot, x):
        if slot:
            R.give[name][hl] = x.astype(BF16)
            start(remote(R.give[name].at[hl], R.take[name].at[hl], "fin", (index, hl), sibling))
        else:
            put_rows(flat, core * mine + hl, x)

    def total_q(slot, hl):
        extra = None
        for level in reversed(range(levels)):
            if level == 4:
                x = R.dq4in[hl, pl.ds(16 * slot, 16)].astype(F32)
            else:
                x = R.st_dq[slot, hl, plan.span(level)]
            if level > 4:
                x = run_sums(x, level - 4)
            x = x * 0.5**level
            if extra is None:
                extra = x
            else:
                extra = x + (extra if extra.shape[0] == x.shape[0] else twice(extra))
        return extra * factor

    def total_kv(slot, hl, which):
        extra = R.back[4][hl, slot, which].astype(F32) * 0.5**4
        for level in high:
            x = R.back[level][0, slot, hl, which].astype(F32)
            for j in range(1, plan.chips(level)):
                x = x + R.back[level][j, slot, hl, which].astype(F32)
            extra = extra + run_sums(x, level - 4) * 0.5**level
        x = R.back[3][hl, 0, slot, which].astype(F32)
        if hl in straight:
            x = x + R.back[3][hl, 1, slot, which].astype(F32)
        extra = x * 0.5**3 + twice(extra)
        extra = R.back[2][hl, slot, which].astype(F32) * 0.5**2 + twice(extra)
        x = (R.dk, R.dv)[which][slot, hl] + twice(twice(extra))
        return x if which else x * factor

    def collect(index, name, flat):
        for hl in range(mine):
            arrived(R.take[name].at[hl], "fin", (index, hl))
            put_rows(flat, (1 - core) * mine + hl, R.take[name][hl].astype(F32))

        def body(i, carry):
            x = R.flat[flat][pl.ds(i * pitch, CHUNK * heads), :]
            outs[index][pl.ds(i * CHUNK, CHUNK)] = x.reshape(CHUNK, heads, width).astype(BF16)
            return carry

        lax.fori_loop(0, chunks, body, 0)

    in_pairs(local_forward)
    derive(0)
    step_a(0)
    forward4()
    derive(1)
    step_a(1)
    for d in range(2):
        arrived(R.got[3].at[d], "3", d)
    derive(2)
    step_a(2)
    derive(3)
    step_a(3)
    step_f(0)
    high_forward()
    arrived(R.g.at[1], "ex", 3)
    take4()
    step_m(0)
    step_b(0)
    step_c(0)
    step_f(1)
    step_m(1)
    step_f(2)
    step_m(2)
    step_f(3)
    step_m(3)
    share4()
    for hl in range(mine):
        start(remote(R.give["o"].at[hl], R.take["o"].at[hl], "fin", (0, hl), sibling))
    step_b(1)
    step_c(1)
    step_b(2)
    step_c(2)
    step_b(3)
    step_c(3)
    collect(0, "o", "g")
    high_backward()
    backward4()
    in_pairs(local_backward)
    flush(7)
    for i in range(1, 4):
        arrived(R.dq4in.at[turned[i]], "x4", i)
    for hl in range(mine):
        hand(1, "dq", "q", hl, 1, total_q(1, hl))
    for i in range(4):
        arrived(R.back[4].at[turned[i]], "b4", i)
    for level in high:
        for j in range(plan.chips(level)):
            arrived(R.back[level].at[j], "r" + str(level), j)
    for hl in range(mine):
        arrived(R.back[2].at[hl], "b2", hl)
        for block in range(2):
            if block == 0 or hl in straight:
                arrived(R.back[3].at[hl, block], "b3", (hl, block))
        for which, name in enumerate("kv"):
            hand(2 + which, "d" + name, name, hl, 1, total_kv(1, hl, which))
    for hl in range(mine):
        hand(1, "dq", "q", hl, 0, total_q(0, hl))
        for which, name in enumerate("kv"):
            hand(2 + which, "d" + name, name, hl, 0, total_kv(0, hl, which))
    collect(1, "dq", "q")
    collect(2, "dk", "k")
    collect(3, "dv", "v")
    for copy in sent:
        copy.wait_send()


def hand_over(*refs):
    held, made, leave = refs[:4], refs[4:8], refs[8]
    outward = [pltpu.make_async_copy(held[i], made[i], leave.at[i]) for i in range(4)]
    for copy in outward:
        copy.start()
    for copy in outward:
        copy.wait()


def on_device(query_rows, key_rows, value_rows, out_grad):
    rows, heads, width = query_rows.shape
    plan = Plan(rows, heads, width, lax.axis_size("seq"))
    whole = pl.BlockSpec(memory_space=pl.ANY)
    vmem = pl.BlockSpec(memory_space=pltpu.VMEM)
    out = jax.ShapeDtypeStruct(query_rows.shape, BF16)
    made = pl.pallas_call(
        partial(kernel, plan),
        out_shape=(pltpu.VMEM(query_rows.shape, BF16),) * 4,
        in_specs=[whole] * 4,
        out_specs=(vmem,) * 4,
        scratch_shapes=plan.scratch(),
        compiler_params=pltpu.CompilerParams(
            collective_id=0, has_side_effects=True, vmem_limit_bytes=54 << 20
        ),
    )(query_rows, key_rows, value_rows, out_grad)
    return pl.pallas_call(
        hand_over,
        out_shape=(out, out, out, out),
        in_specs=[vmem] * 4,
        out_specs=(whole,) * 4,
        scratch_shapes=[pltpu.SemaphoreType.DMA((4,))],
    )(*[pltpu.with_memory_space_constraint(x, pltpu.VMEM) for x in made])


def solution(mesh):
    spec = P(("groups", "seq"), None, None)
    return jax.shard_map(
        on_device,
        mesh=mesh,
        in_specs=(spec,) * 4,
        out_specs=(spec,) * 4,
        check_vma=False,
    )
```
